32 devices in a mesh: half: 1, grp: 4 (over y, core), dev: 8 (over z, x).
Axes of the slice: x: 2, y: 2, z: 4, core: 2. Of those that a mesh axis runs over, the one named last changes fastest.
Arguments:
- panel_block: float32 [2048, 512], P(('half', 'grp', 'dev')), may hold values from -1 to 1, as said below
- trailing: float32 [2048, 1024], P(('half', 'grp'), 'dev'), may hold values from -6 to 6
Outputs:
- triangle: float32 [512, 512], replicated
- projected: float32 [512, 1024], P(None, 'dev')
- remainder: float32 [2048, 1024], P(('half', 'grp'), 'dev')
The draws below stay inside these ranges and needn't reach their ends.
Inputs may be any that keep to these rules, and one draw needn't show every extreme that they name: `panel_block`: of full column rank.
All inputs are finite; a program needn't handle non-finite values.
Results may differ from the reference program's by a relative error of at most 0.0003.
Values sent between devices are 32-bit elements; how exact they have to be, the bound alone decides.
A program may use at most 64 MiB of HBM per device.

```python
import jax
import jax.numpy as jnp
from jax import lax

P_SIZE = 512
ROWS = 2048
SLAB = 1024


def draw_panel_block(key, part):
    first = jax.random.fold_in(key, 11)
    second = jax.random.fold_in(key, 23)
    values = jnp.clip(jax.random.normal(first, (ROWS, P_SIZE), jnp.float32), -6.0, 6.0)
    position = jnp.arange(ROWS, dtype=jnp.float32) / ROWS
    row_scale = (3.0 ** position)[:, None] * jax.random.uniform(second, (ROWS, 1), jnp.float32, 0.7, 1.3)
    values = values * row_scale / jnp.sqrt(jnp.float32(ROWS))
    return jnp.clip(values, -1.0, 1.0)


def block_scale(rng, extent, split, least, largest):
    factor_of = 1.0
    for dim, blocks in split:
        steps = jax.random.uniform(jax.random.fold_in(jax.random.fold_in(rng, 6), dim), (blocks,), jnp.float32, least / len(split), largest / len(split))
        factor_of = factor_of * jnp.repeat(jnp.exp(steps), extent[dim] // blocks).reshape((-1,) + (1,) * (len(extent) - 1 - dim))
    return factor_of


def normal_values(stream_key, extent, width, limit, pieces=(), kind=jnp.bfloat16):
    gain = block_scale(stream_key, extent, pieces, -0.22, 0.18) if pieces else 1.0
    values = jax.random.normal(stream_key, extent, jnp.float32) * width * gain
    return jnp.minimum(jnp.maximum(values, -limit), limit).astype(kind)


def setup_inputs(seed: int = 0) -> dict:
    arg_keys = jax.random.split(jax.random.key(seed), 3)
    panel_block = draw_panel_block(jax.random.fold_in(arg_keys[2], 71), 0)
    trailing = normal_values(arg_keys[1], (ROWS, SLAB), 1.0, 6.0, ((0, 4), (1, 8)), jnp.float32)
    return {"panel_block": panel_block, "trailing": trailing}


def reference(panel_block, trailing):
    orthonormal, upper_part = jnp.linalg.qr(panel_block)
    signs = jnp.sign(jnp.diagonal(upper_part))
    triangle = upper_part * signs[:, None]
    orthonormal = orthonormal * signs[None, :]
    projected = jnp.dot(orthonormal.T, trailing, precision=lax.Precision.HIGHEST)
    remainder = trailing - jnp.dot(orthonormal, projected, precision=lax.Precision.HIGHEST)
    return (triangle, projected, remainder)
```

```python
import functools

import jax
import jax.numpy as jnp
from jax import lax
from jax.experimental import pallas as pl
from jax.experimental.pallas import tpu as pltpu
from jax.sharding import PartitionSpec as P

NB = 128
SUB = 8
PAIR = 2
F32 = jnp.float32
BF16 = jnp.bfloat16
LEFT = (0, 0, 1, 0, 1, 2)
RIGHT = (0, 1, 0, 2, 1, 0)


def split(x):
    high = x.astype(BF16)
    rest = x - high.astype(F32)
    middle = rest.astype(BF16)
    low = (rest - middle.astype(F32)).astype(BF16)
    return high, middle, low


def wide(parts, which, axis):
    return jnp.concatenate([parts[s] for s in which], axis=axis)


def contract(a, b, dim):
    return lax.dot_general(a, b, (((1,), (dim,)), ((), ())), preferred_element_type=F32)


def mm(a, b):
    return contract(wide(a, LEFT, 1), wide(b, RIGHT, 0), 0)


def mm_nt(a, b):
    return contract(wide(a, LEFT, 1), wide(b, RIGHT, 1), 1)


def lanes_of(x, at):
    return jnp.take_along_axis(x, jnp.full(x.shape, at, jnp.int32), axis=1)


def factor_block(block, upper_ref, inverse_ref, row0, col0, hook):
    tile = (SUB, NB)
    lane = lax.broadcasted_iota(jnp.int32, tile, 1)
    row = lax.broadcasted_iota(jnp.int32, tile, 0)
    here = [row == j for j in range(SUB)]
    block = list(block)
    groups = len(block)
    ups, lows = [], []
    for b in range(groups):
        hook(b)
        c0 = SUB * b
        own = block[b]
        near = min(groups, (b // PAIR + 2) * PAIR)
        inside = (lane >= c0) & (lane < c0 + SUB)
        cols = [lanes_of(own, c0 + t) for t in range(SUB)]
        columns = {g: [lanes_of(block[g], c0 + t) for t in range(SUB)] for g in range(b + 1, near)}
        v = jnp.where(inside, jnp.where(lane == row + c0, 1.0, 0.0), own)
        w = own
        up = low = None
        for j in range(SUB):
            top = [jnp.broadcast_to(cols[t][j:j + 1, :], tile) if t >= j else None
                   for t in range(SUB)]
            rs = lax.rsqrt(top[j])
            r = rs * rs
            e = cols[j] * r
            vj = jnp.broadcast_to(v[j:j + 1, :], tile)
            wj = jnp.broadcast_to(w[j:j + 1, :], tile)
            vs, ws = vj * rs, wj * rs
            up = ws if j == 0 else jnp.where(here[j], ws, up)
            low = vs if j == 0 else jnp.where(here[j], vs, low)
            v = jnp.where(here[j], vj * r, v - e * vj)
            if j + 1 < SUB:
                w = w - e * wj
            for t in range(j + 1, SUB):
                cols[t] = jnp.where(here[j], top[t] * r, cols[t] - (cols[j] * top[t]) * r)
        up = jnp.where(lane >= row + c0, up, 0.0)
        low = jnp.where(lane <= row + c0, low, 0.0)
        upper_ref[row0 + c0:row0 + c0 + SUB, col0:col0 + NB] = up
        inverse_ref[row0 + c0:row0 + c0 + SUB, :] = low
        ups.append(up)
        lows.append(low)
        if b + 1 < near:
            vt = [jnp.broadcast_to(v[t:t + 1, :], tile) for t in range(SUB)]
        for g in range(b + 1, near):
            terms = [columns[g][t] * vt[t] for t in range(SUB)]
            while len(terms) > 1:
                terms = [terms[i] + terms[i + 1] for i in range(0, len(terms), 2)]
            block[g] = jnp.where(inside, 0.0, block[g]) - terms[0]
        if (b + 1) % PAIR == 0 and near < groups:
            end = c0 + SUB
            past = lane >= end
            us = jnp.concatenate([jnp.where(past, u, 0.0) for u in ups[-PAIR:]], axis=0)
            vs = jnp.concatenate(
                [jnp.where(past, u, x) for u, x in zip(ups[-PAIR:], lows[-PAIR:])], axis=0)
            res = lax.dot_general(
                wide(split(us), LEFT, 0), wide(split(vs), RIGHT, 0), (((0,), (0,)), ((), ())),
                preferred_element_type=F32)
            done = (lane >= end - PAIR * SUB) & (lane < end)
            for g in range(near, groups):
                block[g] = jnp.where(done, 0.0, block[g]) - res[SUB * g:SUB * (g + 1), :]


def packing(p, n):
    blocks = p // NB
    where, stretch = {}, []
    at = 0
    for j in range(blocks):
        first = at
        for i in range(j + 1):
            where["gram", i, j] = at
            at += NB
        for i in ((j,) if j > 1 else (0, 1) if j == 1 else (0,) if blocks == 1 else ()):
            for q in range(n // NB):
                where["cross", i, q] = at
                at += NB
        stretch.append((first, at - first))
    return where, stretch, at


def fused_kernel(halves, groups, devs, panel_hbm, trailing_hbm, triangle_ref, projected_ref,
                 remainder_ref, panel, slab, total, inbox, work, inverse, panel3, turned3, slab3,
                 upper3, upper_t3, inverse3, inverse_t3, projected3, both3, y3,
                 l_sem, a_send, a_recv, b_send, b_recv, r_send, r_recv):
    mesh_ids = pl.DeviceIdType.MESH
    mine = lax.axis_index("dev")
    rank = lax.axis_index("half") * groups + lax.axis_index("grp")
    pairs = devs // 2
    pair, parity = mine // 2, mine % 2
    levels = (halves * groups).bit_length() - 1
    blocks, size, _ = panel.shape
    rows = size // devs
    p = blocks * NB
    n = slab.shape[1]
    last = blocks - 1
    where, stretch, _ = packing(p, n)

    def slot(dev):
        return pl.ds(pl.multiple_of(dev * rows, rows), rows)

    def same(step):
        return ((pair + step) % pairs) * 2 + parity

    def at_rank(level):
        bit = 1 << level
        other = rank + bit * (1 - 2 * ((rank // bit) % 2))
        return {"half": other // groups, "grp": other % groups}

    def blk(i):
        return slice(i * NB, (i + 1) * NB)

    loads = [pltpu.make_async_copy(panel_hbm.at[:, blk(j)], panel.at[j, slot(mine)], l_sem.at[j])
             for j in range(blocks)]
    loads.append(pltpu.make_async_copy(trailing_hbm, slab, l_sem.at[blocks]))
    for copy in loads:
        copy.start()

    beside = pair * 2 + 1 - parity
    peers = [{"dev": same(step)} for step in range(1, pairs)] + [{"dev": beside}]
    peers += [at_rank(level) for level in range(levels)]
    barrier = pltpu.get_barrier_semaphore()
    for peer in peers:
        pl.semaphore_signal(barrier, inc=1, device_id=peer, device_id_type=mesh_ids)
    pl.semaphore_wait(barrier, len(peers))

    first, onward = {}, {}
    for j in range(blocks):
        for step in range(1, pairs):
            first[j, step] = pltpu.make_async_remote_copy(
                src_ref=panel.at[j, slot(mine)], dst_ref=panel.at[j, slot(mine)],
                send_sem=a_send.at[j, step], recv_sem=a_recv.at[j, step],
                device_id={"dev": same(step)}, device_id_type=mesh_ids)
        for step in range(pairs):
            owner = same(pairs - step)
            onward[j, step] = pltpu.make_async_remote_copy(
                src_ref=panel.at[j, slot(owner)], dst_ref=panel.at[j, slot(owner)],
                send_sem=b_send.at[j, step], recv_sem=b_recv.at[j, step],
                device_id={"dev": beside}, device_id_type=mesh_ids)
    for j in range(blocks):
        loads[j].wait()
        for step in range(1, pairs):
            first[j, step].start()
        onward[j, 0].start()

    def forward(j):
        for step in range(1, pairs):
            first[j, step].wait_recv()
            onward[j, step].start()

    def reduction(j, level):
        begin, count = stretch[j]
        half = count // 2
        low = begin + (rank % 2) * half
        keep = pl.ds(pl.multiple_of(low, 8), half)
        give = pl.ds(pl.multiple_of(2 * begin + half - low, 8), half)
        copy = pltpu.make_async_remote_copy(
            src_ref=total.at[keep if level else give],
            dst_ref=inbox.at[level, pl.ds(begin // 2, half)],
            send_sem=r_send.at[level, j], recv_sem=r_recv.at[level, j],
            device_id=at_rank(level if level < levels else 0), device_id_type=mesh_ids)
        return copy, keep, give, slice(begin // 2, begin // 2 + half)

    def arrive(j):
        for step in range(pairs):
            onward[j, step].wait_recv()

    def prepare(j):
        x = panel[j]
        for s, part in enumerate(split(x)):
            panel3[s, j] = part
        for s, part in enumerate(split(x.T)):
            turned3[s, blk(j), :] = part

    def products(i, j):
        at = where["gram", i, j]
        total[at:at + NB, :] = mm([turned3[s, blk(i), :] for s in range(3)],
                                  [panel3[s, j] for s in range(3)])

    def crossed(i):
        out = mm([turned3[s, blk(i), :] for s in range(3)], [slab3[s] for s in range(3)])
        for q in range(n // NB):
            at = where["cross", i, q]
            total[at:at + NB, :] = out[:, blk(q)]

    def gram(j):
        prepare(j)
        for i in range(j + 1):
            products(i, j)
        if j > 1:
            crossed(j)
        elif j == 1:
            crossed(1)
        elif blocks == 1:
            load_slab()
            crossed(0)

    def load_slab():
        loads[blocks].wait()
        for s, part in enumerate(split(slab[...])):
            slab3[s] = part

    def begin(j):
        arrive(j)
        gram(j)
        reduction(j, 0)[0].start()
        if j == 0 and blocks > 1:
            load_slab()
            crossed(0)

    def advance(j, level):
        copy, keep, give, place = reduction(j, level)
        copy.wait()
        if level < levels:
            total[keep, :] += inbox[level, place]
            reduction(j, level + 1)[0].start()
        else:
            total[give, :] = inbox[level, place]

    queue = []
    for j in range(blocks):
        queue.append((2 * j, j, functools.partial(begin, j), None))
        for level in range(levels + 1):
            queue.append((2 * j + 1 + level, j, functools.partial(advance, j, level),
                          j if level == levels else None))
    for j in range(1, blocks):
        queue.append((2 * j - 1.5 if j < 3 else 2 * j - 2.5, j, functools.partial(forward, j), None))
    queue = [(task, end) for _, _, task, end in sorted(queue, key=lambda x: x[:2])]
    ready = set()

    def pump():
        if queue:
            task, end = queue.pop(0)
            task()
            if end is not None:
                ready.add(end)

    def ensure(j):
        while j not in ready:
            pump()

    def gram_of(i, j):
        at = where["gram", i, j]
        return total[at:at + NB, :]

    def cross_of(i):
        pieces = [where["cross", i, q] for q in range(n // NB)]
        return jnp.concatenate([total[at:at + NB, :] for at in pieces], axis=1)

    def put(ref, at, x):
        for s, part in enumerate(split(x)):
            ref[(s, *at)] = part

    def get(ref, *at):
        return [ref[(s, *at)] for s in range(3)]

    def lead(i, j):
        a = gram_of(i, j)
        if i:
            a = a - mm(get(upper_t3, blk(i), slice(0, i * NB)), get(upper3, slice(0, i * NB), blk(j)))
        return a

    def link(a, i, j):
        right = mm(get(inverse3, blk(i)), a[0])
        turned = mm_nt(a[1], get(inverse3, blk(i)))
        triangle_ref[blk(i), blk(j)] = right
        put(upper3, (blk(i), blk(j)), right)
        put(upper_t3, (blk(j), blk(i)), turned)

    def diagonal(j):
        if not j:
            return gram_of(0, 0)
        past = slice(0, j * NB)
        return gram_of(j, j) - mm(get(upper_t3, blk(j), past), get(upper3, past, blk(j)))

    def projection(j):
        d = cross_of(j)
        if j:
            past = slice(0, j * NB)
            d = d - mm(get(upper_t3, blk(j), past), get(projected3, past))
        return d

    forward(0)
    for i in range(1, blocks):
        triangle_ref[blk(i), 0:i * NB] = jnp.zeros((NB, i * NB), F32)

    def project(j):
        out = mm(get(inverse3, blk(j)), split(projection(j)))
        projected_ref[blk(j), :] = out
        put(projected3, (blk(j),), out)

    def back_substitution():
        for k in reversed(range(last)):
            rhs = jnp.concatenate([projected_ref[blk(k), :], triangle_ref[blk(k), blk(last)]], axis=1)
            if k + 1 < last:
                after = slice((k + 1) * NB, last * NB)
                rhs = rhs - mm(get(upper3, blk(k), after), get(both3, after))
            put(both3, (blk(k),), mm(get(inverse_t3, blk(k)), split(rhs)))

    def reduce_rest():
        rest = jnp.concatenate([slab[...], panel[last]], axis=1)
        if last:
            before = [jnp.concatenate([panel3[s, k] for k in range(last)], axis=1) for s in range(3)]
            rest = rest - mm(before, get(both3, slice(0, last * NB)))
        remainder_ref[...] = rest[:, 0:n]
        put(y3, (), rest[:, n:n + NB])

    for j in range(blocks):
        ensure(j)
        if j:
            for i in range(j):
                if (i, j) not in ready:
                    a = lead(i, j)
                    link((split(a), split(a.T)), i, j)
        work[...] = diagonal(j)
        tasks = []
        if j:
            tasks.append(functools.partial(project, j - 1))
        if j == last:
            tasks += [back_substitution, reduce_rest]

        def hook(b):
            if b and b % 2 == 0:
                pump()
            if b == 1:
                for task in tasks:
                    task()

        factor_block([work[SUB * g:SUB * (g + 1), :] for g in range(NB // SUB)],
                     triangle_ref, inverse, j * NB, j * NB, hook)
        done = inverse[blk(j), :]
        put(inverse3, (blk(j),), done)
        put(inverse_t3, (blk(j),), done.T)
    project(last)
    short = mm(get(inverse_t3, blk(last)), get(projected3, blk(last)))
    remainder_ref[...] = remainder_ref[...] - mm(get(y3), split(short))
    for copy in (*first.values(), *onward.values()):
        copy.wait_send()


def on_device(mesh, panel_block, trailing):
    halves, groups, devs = (mesh.shape[name] for name in ("half", "grp", "dev"))
    rows, p = panel_block.shape
    size, n = trailing.shape
    blocks = p // NB
    _, _, length = packing(p, n)
    levels = (halves * groups).bit_length() - 1
    vmem, dma = pltpu.VMEM, pltpu.SemaphoreType.DMA
    space = pl.BlockSpec(memory_space=pl.ANY)
    inside = pl.BlockSpec(memory_space=pltpu.VMEM)
    return pl.pallas_call(
        functools.partial(fused_kernel, halves, groups, devs),
        out_shape=(
            jax.ShapeDtypeStruct((p, p), F32),
            jax.ShapeDtypeStruct((p, n), F32),
            jax.ShapeDtypeStruct((size, n), F32),
        ),
        in_specs=[space] * 2,
        out_specs=(inside,) * 3,
        scratch_shapes=[
            vmem((blocks, size, NB), F32),
            vmem((size, n), F32),
            vmem((length, NB), F32),
            vmem((levels + 1, length // 2, NB), F32),
            vmem((NB, NB), F32),
            vmem((p, NB), F32),
            vmem((3, blocks, size, NB), BF16),
            vmem((3, p, size), BF16),
            vmem((3, size, n), BF16),
            vmem((3, p, p), BF16),
            vmem((3, p, p), BF16),
            vmem((3, p, NB), BF16),
            vmem((3, p, NB), BF16),
            vmem((3, p, n), BF16),
            vmem((3, p, n + NB), BF16),
            vmem((3, size, NB), BF16),
            dma((blocks + 1,)),
            dma((blocks, devs // 2)), dma((blocks, devs // 2)),
            dma((blocks, devs // 2)), dma((blocks, devs // 2)),
            dma((levels + 1, blocks)), dma((levels + 1, blocks)),
        ],
        compiler_params=pltpu.CompilerParams(collective_id=0, has_side_effects=True),
        name="factor_project",
    )(panel_block, trailing)


def solution(mesh):
    placed = (P(("half", "grp", "dev"), None), P(("half", "grp"), "dev"))
    return jax.shard_map(
        functools.partial(on_device, mesh),
        mesh=mesh,
        in_specs=placed,
        out_specs=(P(), P(None, "dev"), P(("half", "grp"), "dev")),
        check_vma=False,
    )
```

```python
import functools

import jax
import jax.numpy as jnp
from jax import lax
from jax.experimental import pallas as pl
from jax.experimental.pallas import tpu as pltpu
from jax.sharding import PartitionSpec as P

NB = 128
SUB = 8
PAIR = 2
F32 = jnp.float32
BF16 = jnp.bfloat16
LEFT = (0, 0, 1, 0, 1, 2)
RIGHT = (0, 1, 0, 2, 1, 0)


TIMES = {
    ("gram", 0): (12.5, 14.6, 17.3, 18.3),
    ("gram", 1): (16.6, 18.7, 21.4, 22.1),
    ("cross", 1): (19.0, 19.9, 23.4, 24.2),
    ("gram", 2): (20.4, 22.0, 25.9, 26.6),
    ("gram", 3): (23.1, 24.6, 29.4, 30.2),
    ("cross", 2): (24.9, 25.7, 30.0, 30.6),
    ("cross", 3): (27.5, 28.3, 30.9, 31.5),
}
BEGINS = (18.6, 23.0, 27.0, 31.5)


def split(x):
    high = x.astype(BF16)
    rest = x - high.astype(F32)
    middle = rest.astype(BF16)
    low = (rest - middle.astype(F32)).astype(BF16)
    return high, middle, low


def wide(parts, which, axis):
    return jnp.concatenate([parts[s] for s in which], axis=axis)


def contract(a, b, dim):
    return lax.dot_general(a, b, (((1,), (dim,)), ((), ())), preferred_element_type=F32)


def mm(a, b):
    return contract(wide(a, LEFT, 1), wide(b, RIGHT, 0), 0)


def mm_nt(a, b):
    return contract(wide(a, LEFT, 1), wide(b, RIGHT, 1), 1)


def lanes_of(x, at):
    return jnp.take_along_axis(x, jnp.full(x.shape, at, jnp.int32), axis=1)


def factor_block(block, upper_ref, inverse_ref, row0, col0, hook):
    tile = (SUB, NB)
    lane = lax.broadcasted_iota(jnp.int32, tile, 1)
    row = lax.broadcasted_iota(jnp.int32, tile, 0)
    here = [row == j for j in range(SUB)]
    block = list(block)
    groups = len(block)
    ups, lows = [], []
    for b in range(groups):
        hook(b)
        c0 = SUB * b
        own = block[b]
        near = min(groups, (b // PAIR + 2) * PAIR)
        inside = (lane >= c0) & (lane < c0 + SUB)
        cols = [lanes_of(own, c0 + t) for t in range(SUB)]
        columns = {g: [lanes_of(block[g], c0 + t) for t in range(SUB)] for g in range(b + 1, near)}
        v = jnp.where(inside, jnp.where(lane == row + c0, 1.0, 0.0), own)
        w = own
        up = low = None
        for j in range(SUB):
            top = [jnp.broadcast_to(cols[t][j:j + 1, :], tile) if t >= j else None
                   for t in range(SUB)]
            rs = lax.rsqrt(top[j])
            r = rs * rs
            e = cols[j] * r
            vj = jnp.broadcast_to(v[j:j + 1, :], tile)
            wj = jnp.broadcast_to(w[j:j + 1, :], tile)
            vs, ws = vj * rs, wj * rs
            up = ws if j == 0 else jnp.where(here[j], ws, up)
            low = vs if j == 0 else jnp.where(here[j], vs, low)
            v = jnp.where(here[j], vj * r, v - e * vj)
            if j + 1 < SUB:
                w = w - e * wj
            for t in range(j + 1, SUB):
                cols[t] = jnp.where(here[j], top[t] * r, cols[t] - (cols[j] * top[t]) * r)
        up = jnp.where(lane >= row + c0, up, 0.0)
        low = jnp.where(lane <= row + c0, low, 0.0)
        upper_ref[row0 + c0:row0 + c0 + SUB, col0:col0 + NB] = up
        inverse_ref[row0 + c0:row0 + c0 + SUB, :] = low
        ups.append(up)
        lows.append(low)
        if b + 1 < near:
            vt = [jnp.broadcast_to(v[t:t + 1, :], tile) for t in range(SUB)]
        for g in range(b + 1, near):
            terms = [columns[g][t] * vt[t] for t in range(SUB)]
            while len(terms) > 1:
                terms = [terms[i] + terms[i + 1] for i in range(0, len(terms), 2)]
            block[g] = jnp.where(inside, 0.0, block[g]) - terms[0]
        if (b + 1) % PAIR == 0 and near < groups:
            end = c0 + SUB
            past = lane >= end
            us = jnp.concatenate([jnp.where(past, u, 0.0) for u in ups[-PAIR:]], axis=0)
            vs = jnp.concatenate(
                [jnp.where(past, u, x) for u, x in zip(ups[-PAIR:], lows[-PAIR:])], axis=0)
            res = lax.dot_general(
                wide(split(us), LEFT, 0), wide(split(vs), RIGHT, 0), (((0,), (0,)), ((), ())),
                preferred_element_type=F32)
            done = (lane >= end - PAIR * SUB) & (lane < end)
            for g in range(near, groups):
                block[g] = jnp.where(done, 0.0, block[g]) - res[SUB * g:SUB * (g + 1), :]


def packing(p, n):
    blocks = p // NB
    regions = [("gram", (0,))]
    for j in range(1, blocks):
        regions.append(("gram", (j,)))
        regions.append(("cross", (0, 1) if j == 1 else (j,)))
    if blocks == 1:
        regions.append(("cross", (0,)))
    where, stretch = {}, {}
    at = 0
    for kind, members in regions:
        first = at
        for j in members:
            for i in range(j + 1 if kind == "gram" else n // NB):
                where[(kind, i, j) if kind == "gram" else (kind, j, i)] = at
                at += NB
        stretch[kind, members[-1]] = (first, at - first)
    return where, stretch, at


def fused_kernel(halves, groups, devs, panel_hbm, trailing_hbm, triangle_ref, projected_ref,
                 remainder_ref, panel, slab, total, inbox, work, inverse, panel3, turned3, slab3,
                 upper3, upper_t3, inverse3, inverse_t3, projected3, both3, y3,
                 l_sem, a_send, a_recv, b_send, b_recv, r_send, r_recv):
    mesh_ids = pl.DeviceIdType.MESH
    mine = lax.axis_index("dev")
    rank = lax.axis_index("half") * groups + lax.axis_index("grp")
    pairs = devs // 2
    pair, parity = mine // 2, mine % 2
    levels = (halves * groups).bit_length() - 1
    blocks, size, _ = panel.shape
    rows = size // devs
    p = blocks * NB
    n = slab.shape[1]
    last = blocks - 1
    where, stretch, _ = packing(p, n)

    def slot(dev):
        return pl.ds(pl.multiple_of(dev * rows, rows), rows)

    def same(step):
        return ((pair + step) % pairs) * 2 + parity

    def at_rank(level):
        bit = 1 << level
        other = rank + bit * (1 - 2 * ((rank // bit) % 2))
        return {"half": other // groups, "grp": other % groups}

    def blk(i):
        return slice(i * NB, (i + 1) * NB)

    loads = [pltpu.make_async_copy(panel_hbm.at[:, blk(j)], panel.at[j, slot(mine)], l_sem.at[j])
             for j in range(blocks)]
    loads.append(pltpu.make_async_copy(trailing_hbm, slab, l_sem.at[blocks]))
    for copy in loads:
        copy.start()

    beside = pair * 2 + 1 - parity
    peers = [{"dev": same(step)} for step in range(1, pairs)] + [{"dev": beside}]
    peers += [at_rank(level) for level in range(levels)]
    barrier = pltpu.get_barrier_semaphore()
    for peer in peers:
        pl.semaphore_signal(barrier, inc=1, device_id=peer, device_id_type=mesh_ids)
    pl.semaphore_wait(barrier, len(peers))

    first, onward = {}, {}
    for j in range(blocks):
        for step in range(1, pairs):
            first[j, step] = pltpu.make_async_remote_copy(
                src_ref=panel.at[j, slot(mine)], dst_ref=panel.at[j, slot(mine)],
                send_sem=a_send.at[j, step], recv_sem=a_recv.at[j, step],
                device_id={"dev": same(step)}, device_id_type=mesh_ids)
        for step in range(pairs):
            owner = same(pairs - step)
            onward[j, step] = pltpu.make_async_remote_copy(
                src_ref=panel.at[j, slot(owner)], dst_ref=panel.at[j, slot(owner)],
                send_sem=b_send.at[j, step], recv_sem=b_recv.at[j, step],
                device_id={"dev": beside}, device_id_type=mesh_ids)
    for j in range(blocks):
        loads[j].wait()
        for step in range(1, pairs):
            first[j, step].start()
        if j < 2:
            onward[j, 0].start()

    def forward(j):
        for step in range(1, pairs):
            first[j, step].wait_recv()
            onward[j, step].start()
        if j + 2 < blocks:
            onward[j + 2, 0].start()

    names = list(stretch)

    def reduction(name, level):
        begin, count = stretch[name]
        which = names.index(name)
        half = count // 2
        low = begin + (rank % 2) * half
        keep = pl.ds(pl.multiple_of(low, 8), half)
        give = pl.ds(pl.multiple_of(2 * begin + half - low, 8), half)
        copy = pltpu.make_async_remote_copy(
            src_ref=total.at[keep if level else give],
            dst_ref=inbox.at[level, pl.ds(begin // 2, half)],
            send_sem=r_send.at[level, which], recv_sem=r_recv.at[level, which],
            device_id=at_rank(level if level < levels else 0), device_id_type=mesh_ids)
        return copy, keep, give, slice(begin // 2, begin // 2 + half)

    def arrive(j):
        for step in range(pairs):
            onward[j, step].wait_recv()

    def prepare(j):
        x = panel[j]
        for s, part in enumerate(split(x)):
            panel3[s, j] = part
        for s, part in enumerate(split(x.T)):
            turned3[s, blk(j), :] = part

    def products(i, j):
        at = where["gram", i, j]
        total[at:at + NB, :] = mm([turned3[s, blk(i), :] for s in range(3)],
                                  [panel3[s, j] for s in range(3)])

    def crossed(i):
        out = mm([turned3[s, blk(i), :] for s in range(3)], [slab3[s] for s in range(3)])
        for q in range(n // NB):
            at = where["cross", i, q]
            total[at:at + NB, :] = out[:, blk(q)]

    def begin_gram(j):
        arrive(j)
        prepare(j)
        for i in range(j + 1):
            products(i, j)
        reduction(("gram", j), 0)[0].start()

    def begin_cross(j):
        if j < 2:
            loads[blocks].wait()
            for s, part in enumerate(split(slab[...])):
                slab3[s] = part
        for i in range(0 if j < 2 else j, j + 1):
            crossed(i)
        reduction(("cross", j), 0)[0].start()

    def advance(name, level):
        copy, keep, give, place = reduction(name, level)
        copy.wait()
        if level < levels:
            total[keep, :] += inbox[level, place]
            reduction(name, level + 1)[0].start()
        else:
            total[give, :] = inbox[level, place]
            ready.add(name)

    queue = []
    for j in range(1, blocks):
        queue.append((12.4 + 3.0 * (j - 1), functools.partial(forward, j)))
    for name in names:
        first_at, *at = TIMES.get(name, (30.0, 31.0, 32.0, 33.0))
        begin = begin_gram if name[0] == "gram" else begin_cross
        queue.append((first_at, functools.partial(begin, name[1])))
        for level in range(levels + 1):
            place = 0 if level == 0 else 2 if level == levels else 1
            queue.append((at[place], functools.partial(advance, name, level)))
    queue.sort(key=lambda x: x[0])
    ready = set()

    def pump(until):
        while queue and queue[0][0] <= until:
            queue.pop(0)[1]()

    def ensure(name):
        while name not in ready:
            queue.pop(0)[1]()

    def gram_of(i, j):
        at = where["gram", i, j]
        return total[at:at + NB, :]

    def cross_of(i):
        pieces = [where["cross", i, q] for q in range(n // NB)]
        return jnp.concatenate([total[at:at + NB, :] for at in pieces], axis=1)

    def put(ref, at, x):
        for s, part in enumerate(split(x)):
            ref[(s, *at)] = part

    def get(ref, *at):
        return [ref[(s, *at)] for s in range(3)]

    def lead(i, j):
        a = gram_of(i, j)
        if i:
            a = a - mm(get(upper_t3, blk(i), slice(0, i * NB)), get(upper3, slice(0, i * NB), blk(j)))
        return a

    def link(a, i, j):
        right = mm(get(inverse3, blk(i)), a[0])
        turned = mm_nt(a[1], get(inverse3, blk(i)))
        triangle_ref[blk(i), blk(j)] = right
        put(upper3, (blk(i), blk(j)), right)
        put(upper_t3, (blk(j), blk(i)), turned)

    def diagonal(j):
        if not j:
            return gram_of(0, 0)
        past = slice(0, j * NB)
        return gram_of(j, j) - mm(get(upper_t3, blk(j), past), get(upper3, past, blk(j)))

    def projection(j):
        d = cross_of(j)
        if j:
            past = slice(0, j * NB)
            d = d - mm(get(upper_t3, blk(j), past), get(projected3, past))
        return d

    forward(0)
    for i in range(1, blocks):
        triangle_ref[blk(i), 0:i * NB] = jnp.zeros((NB, i * NB), F32)

    def project(j):
        out = mm(get(inverse3, blk(j)), split(projection(j)))
        projected_ref[blk(j), :] = out
        put(projected3, (blk(j),), out)

    def reduce_rest():
        for k in reversed(range(last)):
            rhs = jnp.concatenate([projected_ref[blk(k), :], triangle_ref[blk(k), blk(last)]], axis=1)
            if k + 1 < last:
                after = slice((k + 1) * NB, last * NB)
                rhs = rhs - mm(get(upper3, blk(k), after), get(both3, after))
            put(both3, (blk(k),), mm(get(inverse_t3, blk(k)), split(rhs)))
        rest = jnp.concatenate([slab[...], panel[last]], axis=1)
        if last:
            before = [jnp.concatenate([panel3[s, k] for k in range(last)], axis=1) for s in range(3)]
            rest = rest - mm(before, get(both3, slice(0, last * NB)))
        remainder_ref[...] = rest[:, 0:n]
        put(y3, (), rest[:, n:n + NB])

    def project_at(i):
        ensure(("cross", max(i, min(1, last))))
        project(i)

    for j in range(blocks):
        ensure(("gram", j))
        for i in range(j):
            a = lead(i, j)
            link((split(a), split(a.T)), i, j)
        work[...] = diagonal(j)

        def hook(b):
            pump(BEGINS[min(j, 3)] + 0.2 * b)
            if j == last:
                if b == 1:
                    if j:
                        project_at(j - 1)
                    reduce_rest()
            elif j and b == 11 - 8 * (j > 1):
                project_at(j - 1)

        factor_block([work[SUB * g:SUB * (g + 1), :] for g in range(NB // SUB)],
                     triangle_ref, inverse, j * NB, j * NB, hook)
        done = inverse[blk(j), :]
        put(inverse3, (blk(j),), done)
        put(inverse_t3, (blk(j),), done.T)
    ensure(("cross", last))
    project(last)
    short = mm(get(inverse_t3, blk(last)), get(projected3, blk(last)))
    remainder_ref[...] = remainder_ref[...] - mm(get(y3), split(short))
    for copy in (*first.values(), *onward.values()):
        copy.wait_send()


def on_device(mesh, panel_block, trailing):
    halves, groups, devs = (mesh.shape[name] for name in ("half", "grp", "dev"))
    rows, p = panel_block.shape
    size, n = trailing.shape
    blocks = p // NB
    _, stretch, length = packing(p, n)
    levels = (halves * groups).bit_length() - 1
    vmem, dma = pltpu.VMEM, pltpu.SemaphoreType.DMA
    space = pl.BlockSpec(memory_space=pl.ANY)
    inside = pl.BlockSpec(memory_space=pltpu.VMEM)
    return pl.pallas_call(
        functools.partial(fused_kernel, halves, groups, devs),
        out_shape=(
            pltpu.VMEM((p, p), F32),
            pltpu.VMEM((p, n), F32),
            pltpu.VMEM((size, n), F32),
        ),
        in_specs=[space] * 2,
        out_specs=(inside,) * 3,
        scratch_shapes=[
            vmem((blocks, size, NB), F32),
            vmem((size, n), F32),
            vmem((length, NB), F32),
            vmem((levels + 1, length // 2, NB), F32),
            vmem((NB, NB), F32),
            vmem((p, NB), F32),
            vmem((3, blocks, size, NB), BF16),
            vmem((3, p, size), BF16),
            vmem((3, size, n), BF16),
            vmem((3, p, p), BF16),
            vmem((3, p, p), BF16),
            vmem((3, p, NB), BF16),
            vmem((3, p, NB), BF16),
            vmem((3, p, n), BF16),
            vmem((3, p, n + NB), BF16),
            vmem((3, size, NB), BF16),
            dma((blocks + 1,)),
            dma((blocks, devs // 2)), dma((blocks, devs // 2)),
            dma((blocks, devs // 2)), dma((blocks, devs // 2)),
            dma((levels + 1, len(stretch))), dma((levels + 1, len(stretch))),
        ],
        compiler_params=pltpu.CompilerParams(collective_id=0, has_side_effects=True),
        name="factor_project",
    )(panel_block, trailing)


def solution(mesh):
    placed = (P(("half", "grp", "dev"), None), P(("half", "grp"), "dev"))
    return jax.shard_map(
        functools.partial(on_device, mesh),
        mesh=mesh,
        in_specs=placed,
        out_specs=(P(), P(None, "dev"), P(("half", "grp"), "dev")),
        check_vma=False,
    )
```

```python
import functools

import jax
import jax.numpy as jnp
from jax import lax
from jax.experimental import pallas as pl
from jax.experimental.pallas import tpu as pltpu
from jax.sharding import PartitionSpec as P

NB = 128
SUB = 8
PAIR = 2
F32 = jnp.float32
BF16 = jnp.bfloat16
LEFT = (0, 0, 1, 0, 1, 2)
RIGHT = (0, 1, 0, 2, 1, 0)


PLACES = {
    ("gram", 0): ((-12, -12), -10, -7, -5),
    ("gram", 1): ((-6, -6), 4, 15.3, 15.5),
    ("cross", 1): ((1,), 8, 18, 23),
    ("gram", 2): ((6, 7), 14, 23, 26),
    ("gram", 3): ((15.1, 15.2), 19, 36, 40),
    ("cross", 2): ((28,), 31.2, 45, 47.8),
    ("cross", 3): ((33,), 37, 47.6, 47.9),
}
FORWARDS = (0, -11, -9, 0)


def split(x):
    high = x.astype(BF16)
    rest = x - high.astype(F32)
    middle = rest.astype(BF16)
    low = (rest - middle.astype(F32)).astype(BF16)
    return high, middle, low


def wide(parts, which, axis):
    return jnp.concatenate([parts[s] for s in which], axis=axis)


def contract(a, b, dim):
    return lax.dot_general(a, b, (((1,), (dim,)), ((), ())), preferred_element_type=F32)


def mm(a, b):
    return contract(wide(a, LEFT, 1), wide(b, RIGHT, 0), 0)


def mm_nt(a, b):
    return contract(wide(a, LEFT, 1), wide(b, RIGHT, 1), 1)


def lanes_of(x, at):
    return jnp.take_along_axis(x, jnp.full(x.shape, at, jnp.int32), axis=1)


def factor_block(block, upper_ref, inverse_ref, row0, col0, hook):
    tile = (SUB, NB)
    lane = lax.broadcasted_iota(jnp.int32, tile, 1)
    row = lax.broadcasted_iota(jnp.int32, tile, 0)
    here = [row == j for j in range(SUB)]
    block = list(block)
    groups = len(block)
    ups, lows = [], []
    following = None

    def one(x, at):
        return jnp.broadcast_to(x[at:at + 1, :], tile)

    for b in range(groups):
        hook(b)
        c0 = SUB * b
        own = block[b]
        near = min(groups, (b // PAIR + 2) * PAIR)
        inside = (lane >= c0) & (lane < c0 + SUB)
        opens = b % PAIR == 0
        cols = [lanes_of(own, c0 + t) for t in range(SUB)] if opens else following
        columns = {g: [lanes_of(block[g], c0 + t) for t in range(SUB)] for g in range(b + 1, near)}
        if opens:
            following = [lanes_of(block[b + 1], c0 + SUB + t) for t in range(SUB)]
            below = list(columns[b + 1])
        v = jnp.where(inside, jnp.where(lane == row + c0, 1.0, 0.0), own)
        w = own
        up = low = None
        raw = list(cols)
        for j in range(SUB):
            top = [one(raw[t], j) if t >= j else None for t in range(SUB)]
            rs = lax.rsqrt(top[j])
            r = rs * rs
            e = cols[j] * r
            vj, wj = one(v, j), one(w, j)
            vs, ws = vj * rs, wj * rs
            up = ws if j == 0 else jnp.where(here[j], ws, up)
            low = vs if j == 0 else jnp.where(here[j], vs, low)
            v = jnp.where(here[j], vj * r, v - e * vj)
            if j + 1 < SUB:
                w = w - e * wj
            for t in range(j + 1, SUB):
                raw[t] = cols[t] - (cols[j] * top[t]) * r
                cols[t] = jnp.where(here[j], top[t] * r, raw[t])
            if opens:
                share = below[j] * r
                for t in range(SUB):
                    following[t] = following[t] - share * one(below[j], t)
                for t in range(j + 1, SUB):
                    below[t] = below[t] - (below[j] * top[t]) * r
        up = jnp.where(lane >= row + c0, up, 0.0)
        low = jnp.where(lane <= row + c0, low, 0.0)
        upper_ref[row0 + c0:row0 + c0 + SUB, col0:col0 + NB] = up
        inverse_ref[row0 + c0:row0 + c0 + SUB, :] = low
        ups.append(up)
        lows.append(low)
        if b + 1 < near:
            vt = [one(v, t) for t in range(SUB)]
        for g in range(b + 1, near):
            terms = [columns[g][t] * vt[t] for t in range(SUB)]
            while len(terms) > 1:
                terms = [terms[i] + terms[i + 1] for i in range(0, len(terms), 2)]
            block[g] = jnp.where(inside, 0.0, block[g]) - terms[0]
        if not opens and near < groups:
            end = c0 + SUB
            past = lane >= end
            us = jnp.concatenate([jnp.where(past, u, 0.0) for u in ups[-PAIR:]], axis=0)
            vs = jnp.concatenate(
                [jnp.where(past, u, x) for u, x in zip(ups[-PAIR:], lows[-PAIR:])], axis=0)
            res = lax.dot_general(
                wide(split(us), LEFT, 0), wide(split(vs), RIGHT, 0), (((0,), (0,)), ((), ())),
                preferred_element_type=F32)
            done = (lane >= end - PAIR * SUB) & (lane < end)
            for g in range(near, groups):
                block[g] = jnp.where(done, 0.0, block[g]) - res[SUB * g:SUB * (g + 1), :]


def packing(p, n):
    blocks = p // NB
    regions = [("gram", (0,))]
    for j in range(1, blocks):
        regions.append(("gram", (j,)))
        regions.append(("cross", (0, 1) if j == 1 else (j,)))
    if blocks == 1:
        regions.append(("cross", (0,)))
    where, stretch = {}, {}
    at = 0
    for kind, members in regions:
        first = at
        for j in members:
            for i in range(j + 1 if kind == "gram" else n // NB):
                where[(kind, i, j) if kind == "gram" else (kind, j, i)] = at
                at += NB
        stretch[kind, members[-1]] = (first, at - first)
    return where, stretch, at


def fused_kernel(halves, groups, devs, panel_hbm, trailing_hbm, triangle_ref, projected_ref,
                 remainder_ref, panel, slab, total, inbox, work, ahead3, inverse, panel3, turned3, slab3,
                 upper3, upper_t3, inverse3, inverse_t3, projected3, both3, y3, last3,
                 l_sem, s_sem, a_recv, b_recv, r_send, r_recv):
    mesh_ids = pl.DeviceIdType.MESH
    mine = lax.axis_index("dev")
    rank = lax.axis_index("half") * groups + lax.axis_index("grp")
    pairs = devs // 2
    pair, parity = mine // 2, mine % 2
    levels = (halves * groups).bit_length() - 1
    blocks, size, _ = panel.shape
    rows = size // devs
    p = blocks * NB
    n = slab.shape[1]
    last = blocks - 1
    where, stretch, _ = packing(p, n)

    def slot(dev):
        return pl.ds(pl.multiple_of(dev * rows, rows), rows)

    def same(step):
        return ((pair + step) % pairs) * 2 + parity

    def at_rank(level):
        bit = 1 << level
        other = rank + bit * (1 - 2 * ((rank // bit) % 2))
        return {"half": other // groups, "grp": other % groups}

    def blk(i):
        return slice(i * NB, (i + 1) * NB)

    for j in range(blocks):
        pltpu.make_async_copy(panel_hbm.at[:, blk(j)], panel.at[j, slot(mine)], l_sem.at[0]).start()
    slab_load = pltpu.make_async_copy(trailing_hbm, slab, l_sem.at[1])
    slab_load.start()

    beside = pair * 2 + 1 - parity
    peers = [{"dev": same(step)} for step in range(1, pairs)] + [{"dev": beside}]
    peers += [at_rank(level) for level in range(levels)]
    barrier = pltpu.get_barrier_semaphore()
    for peer in peers:
        pl.semaphore_signal(barrier, inc=1, device_id=peer, device_id_type=mesh_ids)
    pl.semaphore_wait(barrier, len(peers))

    def arrival(j, step):
        return pltpu.make_async_remote_copy(
            src_ref=panel.at[j, slot(mine)], dst_ref=panel.at[j, slot(mine)],
            send_sem=s_sem.at[0], recv_sem=a_recv.at[j, step - 1],
            device_id={"dev": same(step)}, device_id_type=mesh_ids)

    def passing(j, step):
        owner = same(pairs - step)
        return pltpu.make_async_remote_copy(
            src_ref=panel.at[j, slot(owner)], dst_ref=panel.at[j, slot(owner)],
            send_sem=s_sem.at[1], recv_sem=b_recv.at[j],
            device_id={"dev": beside}, device_id_type=mesh_ids)

    def send(j):
        if j < blocks:
            for step in range(1, pairs):
                arrival(j, step).start()

    own = panel.at[:, slot(mine)]
    pltpu.make_async_copy(own, own, l_sem.at[0]).wait()
    send(0)
    passing(0, 0).start()

    def forward(j):
        near = jnp.minimum(pair, pairs - 1 - pair)
        far = jnp.where(pair < pairs - 1 - pair, 1, -1)
        for k in range(pairs - 1):
            offset = jnp.where(k < 2 * near, (k // 2 + 1) * (1 - 2 * (k % 2)), (k - near + 1) * far)
            step = (pairs - offset) % pairs
            arrival(j, step).wait_recv()
            passing(j, step).start()
            if j == 0 and k == 0:
                send(1)
        send(j + 2)
        if j + 1 < blocks:
            passing(j + 1, 0).start()

    names = list(stretch)

    def reduction(name, level):
        begin, count = stretch[name]
        which = names.index(name)
        half = count // 2
        low = begin + (rank % 2) * half
        keep = pl.ds(pl.multiple_of(low, 8), half)
        give = pl.ds(pl.multiple_of(2 * begin + half - low, 8), half)
        copy = pltpu.make_async_remote_copy(
            src_ref=total.at[keep if level else give],
            dst_ref=inbox.at[level, pl.ds(begin // 2, half)],
            send_sem=r_send.at[level, which], recv_sem=r_recv.at[level, which],
            device_id=at_rank(level if level < levels else 0), device_id_type=mesh_ids)
        return copy, keep, give, slice(begin // 2, begin // 2 + half)

    def together(part, which, at):
        return pltpu.make_async_remote_copy(
            src_ref=part, dst_ref=part, send_sem=s_sem.at[which], recv_sem=b_recv.at[at],
            device_id={"dev": beside}, device_id_type=mesh_ids)

    def arrive(j):
        together(panel.at[j, pl.ds(0, pairs * rows)], 1, j).wait_recv()

    def prepare(j):
        x = panel[j]
        for s, part in enumerate(split(x)):
            panel3[s, j] = part
        for s, part in enumerate(split(x.T)):
            turned3[s, blk(j), :] = part

    def products(j):
        at = where["gram", 0, j]
        total[at:at + (j + 1) * NB, :] = mm([turned3[s, 0:(j + 1) * NB, :] for s in range(3)],
                                            [panel3[s, j] for s in range(3)])

    def crossed(i):
        out = mm([turned3[s, blk(i), :] for s in range(3)], [slab3[s] for s in range(3)])
        for q in range(n // NB):
            at = where["cross", i, q]
            total[at:at + NB, :] = out[:, blk(q)]

    def begin(name):
        reduction(name, 0)[0].start()

    def receive(j):
        arrive(j)
        prepare(j)

    def load_slab():
        slab_load.wait()
        for s, part in enumerate(split(slab[...])):
            slab3[s] = part

    def advance(name, level):
        copy, keep, give, place = reduction(name, level)
        copy.wait()
        if level < levels:
            total[keep, :] += inbox[level, place]
            reduction(name, level + 1)[0].start()
        else:
            total[give, :] = inbox[level, place]
            ready.add(name)

    queue = []

    def add(place, task, *args):
        queue.append((place, functools.partial(task, *args)))

    for j in range(1, blocks):
        add(FORWARDS[min(j, 3)], forward, j)
    for name in names:
        kind, j = name
        start, *at = PLACES.get(name, ((48, 48), 49, 50, 51))
        if kind == "gram":
            add(start[0], receive, j)
            add(start[1], products, j)
        elif j < 2:
            add(-8.5, load_slab)
            add(-8.5, crossed, 0)
        if kind == "cross" and j:
            add(start[0], crossed, j)
        add(start[-1], begin, name)
        for level in range(levels + 1):
            add(at[0 if level == 0 else 2 if level == levels else 1], advance, name, level)
    ready = set()

    def pump(place):
        while queue and queue[0][0] <= place:
            queue.pop(0)[1]()

    def ensure(name):
        at = 0
        while name not in ready:
            while queue[at][1].func is need:
                at += 1
            queue.pop(at)[1]()

    def gram_of(i, j):
        at = where["gram", i, j]
        return total[at:at + NB, :]

    def cross_of(i):
        pieces = [where["cross", i, q] for q in range(n // NB)]
        return jnp.concatenate([total[at:at + NB, :] for at in pieces], axis=1)

    def put(ref, at, x):
        for s, part in enumerate(split(x)):
            ref[(s, *at)] = part

    def get(ref, *at):
        return [ref[(s, *at)] for s in range(3)]

    def lead(i, j):
        a = gram_of(i, j)
        if i:
            a = a - mm(get(upper_t3, blk(i), slice(0, i * NB)), get(upper3, slice(0, i * NB), blk(j)))
        return a

    def link(i, j, a, turned):
        right = mm(get(inverse3, blk(i)), a)
        turned = mm_nt(turned, get(inverse3, blk(i)))
        triangle_ref[blk(i), blk(j)] = right
        put(upper3, (blk(i), blk(j)), right)
        put(upper_t3, (blk(j), blk(i)), turned)

    def early_link(i, j):
        a = lead(i, j)
        link(i, j, split(a), split(a.T))

    def early(j):
        i = j - 1
        a = lead(i, j)
        put(ahead3, (0,), a)
        put(ahead3, (1,), a.T)
        d = gram_of(j, j)
        if i:
            past = slice(0, i * NB)
            d = d - mm(get(upper_t3, blk(j), past), get(upper3, past, blk(j)))
        work[...] = d

    def late(j):
        i = j - 1
        link(i, j, get(ahead3, 0), get(ahead3, 1))
        work[...] -= mm(get(upper_t3, blk(j), blk(i)), get(upper3, blk(i), blk(j)))

    def projection(j):
        d = cross_of(j)
        if j:
            past = slice(0, j * NB)
            d = d - mm(get(upper_t3, blk(j), past), get(projected3, past))
        return d

    forward(0)
    for i in range(1, blocks):
        triangle_ref[blk(i), 0:i * NB] = jnp.zeros((NB, i * NB), F32)

    def project(j):
        out = mm(get(inverse3, blk(j)), split(projection(j)))
        projected_ref[blk(j), :] = out
        put(projected3, (blk(j),), out)

    def solve_back(k):
        rhs = jnp.concatenate([projected_ref[blk(k), :], triangle_ref[blk(k), blk(last)]], axis=1)
        if k + 1 < last:
            after = slice((k + 1) * NB, last * NB)
            rhs = rhs - mm(get(upper3, blk(k), after), get(both3, after))
        put(both3, (blk(k),), mm(get(inverse_t3, blk(k)), split(rhs)))

    def reduce_rest(at):
        rest = jnp.concatenate([slab[at, :], panel[last, at, :]], axis=1)
        if last:
            before = [jnp.concatenate([panel3[s, k, at, :] for k in range(last)], axis=1)
                      for s in range(3)]
            rest = rest - mm(before, get(both3, slice(0, last * NB)))
        remainder_ref[at, :] = rest[:, 0:n]
        put(y3, (at,), rest[:, n:n + NB])

    def need(task, names, *args):
        for name in names:
            ensure(name)
        task(*args)

    for j in range(1, blocks):
        for i in range(j - 1):
            add(16 * j + (-6 if j == 2 else -9) + 3 * i, need, early_link, [("gram", j)], i, j)
        add(16 * j - 1.5, need, early, [("gram", j)], j)
        name = ("cross", max(j - 1, min(1, last)))
        add(16 * j + (8 if j == 1 else 3 if j < last else 1), need, project, [name], j - 1)
    add(16 * last + 1.5, need, lambda: put(last3, (), projection(last)), [("cross", last)])
    for k in range(last):
        add(16 * last + 2 + 2 * k, solve_back, last - 1 - k)
    for r in range(0, size, NB):
        add(16 * last + 4 + 2 * last + 2 * (r // NB), reduce_rest, slice(r, r + NB))
    queue.sort(key=lambda x: x[0])

    for j in range(blocks):
        ensure(("gram", j))
        if j:
            pump(16 * j - 1)
            late(j)
        else:
            work[...] = gram_of(0, 0)
        factor_block([work[SUB * g:SUB * (g + 1), :] for g in range(NB // SUB)],
                     triangle_ref, inverse, j * NB, j * NB, lambda b: pump(16 * j + b))
        done = inverse[blk(j), :]
        put(inverse3, (blk(j),), done)
        if j < last:
            put(inverse_t3, (blk(j),), done.T)
    while queue:
        queue.pop(0)[1]()
    out = mm(get(inverse3, blk(last)), get(last3))
    projected_ref[blk(last), :] = out
    basis = mm_nt(get(y3), get(inverse3, blk(last)))
    remainder_ref[...] = remainder_ref[...] - mm(split(basis), split(out))
    together(panel.at[:, pl.ds(0, (pairs - 1) * rows)], 0, 0).wait_send()
    together(panel.at[:, pl.ds(0, pairs * rows)], 1, 0).wait_send()


def on_device(mesh, panel_block, trailing):
    halves, groups, devs = (mesh.shape[name] for name in ("half", "grp", "dev"))
    rows, p = panel_block.shape
    size, n = trailing.shape
    blocks = p // NB
    _, stretch, length = packing(p, n)
    levels = (halves * groups).bit_length() - 1
    vmem, dma = pltpu.VMEM, pltpu.SemaphoreType.DMA
    space = pl.BlockSpec(memory_space=pl.ANY)
    inside = pl.BlockSpec(memory_space=pltpu.VMEM)
    return pl.pallas_call(
        functools.partial(fused_kernel, halves, groups, devs),
        out_shape=(
            pltpu.VMEM((p, p), F32),
            pltpu.VMEM((p, n), F32),
            pltpu.VMEM((size, n), F32),
        ),
        in_specs=[space] * 2,
        out_specs=(inside,) * 3,
        scratch_shapes=[
            vmem((blocks, size, NB), F32),
            vmem((size, n), F32),
            vmem((length, NB), F32),
            vmem((levels + 1, length // 2, NB), F32),
            vmem((NB, NB), F32),
            vmem((3, 2, NB, NB), BF16),
            vmem((p, NB), F32),
            vmem((3, blocks, size, NB), BF16),
            vmem((3, p, size), BF16),
            vmem((3, size, n), BF16),
            vmem((3, p, p), BF16),
            vmem((3, p, p), BF16),
            vmem((3, p, NB), BF16),
            vmem((3, p, NB), BF16),
            vmem((3, p, n), BF16),
            vmem((3, p, n + NB), BF16),
            vmem((3, size, NB), BF16),
            vmem((3, NB, n), BF16),
            dma((2,)), dma((2,)), dma((blocks, devs // 2 - 1)), dma((blocks,)),
            dma((levels + 1, len(stretch))), dma((levels + 1, len(stretch))),
        ],
        compiler_params=pltpu.CompilerParams(collective_id=0, has_side_effects=True),
        name="factor_project",
    )(panel_block, trailing)


def solution(mesh):
    placed = (P(("half", "grp", "dev"), None), P(("half", "grp"), "dev"))
    return jax.shard_map(
        functools.partial(on_device, mesh),
        mesh=mesh,
        in_specs=placed,
        out_specs=(P(), P(None, "dev"), P(("half", "grp"), "dev")),
        check_vma=False,
    )
```

```python
import functools

import jax
import jax.numpy as jnp
from jax import lax
from jax.experimental import pallas as pl
from jax.experimental.pallas import tpu as pltpu
from jax.sharding import PartitionSpec as P

NB = 128
SUB = 8
PAIR = 2
F32 = jnp.float32
BF16 = jnp.bfloat16
LEFT = (0, 0, 1, 0, 1, 2)
RIGHT = (0, 1, 0, 2, 1, 0)


PLACES = {
    ("gram", 0): ((-12, -12), -10, -7, -5),
    ("gram", 1): ((-6, -6), 2, 15, 15.9),
    ("cross", 1): ((2.1,), 9, 19, 23),
    ("gram", 2): ((6, 7), 13, 24, 28),
    ("gram", 3): ((14.5, 15.2), 18, 35, 39.5),
    ("cross", 2): ((20,), 25, 40, 43),
    ("cross", 3): ((21,), 28.5, 44, 47.9),
}

FORWARDS = (0, -11, -9, 0)


def split(x):
    high = x.astype(BF16)
    rest = x - high.astype(F32)
    middle = rest.astype(BF16)
    low = (rest - middle.astype(F32)).astype(BF16)
    return high, middle, low


def wide(parts, which, axis):
    return jnp.concatenate([parts[s] for s in which], axis=axis)


def contract(a, b, dim):
    return lax.dot_general(a, b, (((1,), (dim,)), ((), ())), preferred_element_type=F32)


def mm(a, b):
    return contract(wide(a, LEFT, 1), wide(b, RIGHT, 0), 0)


def mm_nt(a, b):
    return contract(wide(a, LEFT, 1), wide(b, RIGHT, 1), 1)


def lanes_of(x, at):
    return jnp.take_along_axis(x, jnp.full(x.shape, at, jnp.int32), axis=1)


def factor_block(block, upper_ref, inverse_ref, row0, col0, hook):
    tile = (SUB, NB)
    lane = lax.broadcasted_iota(jnp.int32, tile, 1)
    row = lax.broadcasted_iota(jnp.int32, tile, 0)
    here = [row == j for j in range(SUB)]
    block = list(block)
    groups = len(block)
    ups, lows = [], []
    following = None

    def one(x, at):
        return jnp.broadcast_to(x[at:at + 1, :], tile)

    for b in range(groups):
        hook(b)
        c0 = SUB * b
        own = block[b]
        near = min(groups, (b // PAIR + 2) * PAIR)
        inside = (lane >= c0) & (lane < c0 + SUB)
        opens = b % PAIR == 0
        cols = [lanes_of(own, c0 + t) for t in range(SUB)] if opens else following
        columns = {g: [lanes_of(block[g], c0 + t) for t in range(SUB)] for g in range(b + 1, near)}
        if opens:
            following = [lanes_of(block[b + 1], c0 + SUB + t) for t in range(SUB)]
            below = list(columns[b + 1])
        v = jnp.where(inside, jnp.where(lane == row + c0, 1.0, 0.0), own)
        w = own
        up = low = None
        raw = list(cols)
        for j in range(SUB):
            top = [one(raw[t], j) if t >= j else None for t in range(SUB)]
            rs = lax.rsqrt(top[j])
            r = rs * rs
            e = cols[j] * r
            vj, wj = one(v, j), one(w, j)
            vs, ws = vj * rs, wj * rs
            up = ws if j == 0 else jnp.where(here[j], ws, up)
            low = vs if j == 0 else jnp.where(here[j], vs, low)
            v = jnp.where(here[j], vj * r, v - e * vj)
            if j + 1 < SUB:
                w = w - e * wj
            for t in range(j + 1, SUB):
                raw[t] = cols[t] - (cols[j] * top[t]) * r
                cols[t] = jnp.where(here[j], top[t] * r, raw[t])
            if opens:
                share = below[j] * r
                for t in range(SUB):
                    following[t] = following[t] - share * one(below[j], t)
                for t in range(j + 1, SUB):
                    below[t] = below[t] - (below[j] * top[t]) * r
        up = jnp.where(lane >= row + c0, up, 0.0)
        low = jnp.where(lane <= row + c0, low, 0.0)
        upper_ref[row0 + c0:row0 + c0 + SUB, col0:col0 + NB] = up
        inverse_ref[row0 + c0:row0 + c0 + SUB, :] = low
        ups.append(up)
        lows.append(low)
        if b + 1 < near:
            vt = [one(v, t) for t in range(SUB)]
        for g in range(b + 1, near):
            terms = [columns[g][t] * vt[t] for t in range(SUB)]
            while len(terms) > 1:
                terms = [terms[i] + terms[i + 1] for i in range(0, len(terms), 2)]
            block[g] = jnp.where(inside, 0.0, block[g]) - terms[0]
        if not opens and near < groups:
            end = c0 + SUB
            past = lane >= end
            us = jnp.concatenate([jnp.where(past, u, 0.0) for u in ups[-PAIR:]], axis=0)
            vs = jnp.concatenate(
                [jnp.where(past, u, x) for u, x in zip(ups[-PAIR:], lows[-PAIR:])], axis=0)
            res = lax.dot_general(
                wide(split(us), LEFT, 0), wide(split(vs), RIGHT, 0), (((0,), (0,)), ((), ())),
                preferred_element_type=F32)
            done = (lane >= end - PAIR * SUB) & (lane < end)
            for g in range(near, groups):
                block[g] = jnp.where(done, 0.0, block[g]) - res[SUB * g:SUB * (g + 1), :]


def packing(p, n):
    blocks = p // NB
    regions = [("gram", (0,))]
    for j in range(1, blocks):
        regions.append(("gram", (j,)))
        regions.append(("cross", (0, 1) if j == 1 else (j,)))
    if blocks == 1:
        regions.append(("cross", (0,)))
    where, stretch = {}, {}
    at = 0
    for kind, members in regions:
        first = at
        for j in members:
            for i in range(j + 1 if kind == "gram" else n // NB):
                where[(kind, i, j) if kind == "gram" else (kind, j, i)] = at
                at += NB
        stretch[kind, members[-1]] = (first, at - first)
    return where, stretch, at


def fused_kernel(halves, groups, devs, panel_hbm, trailing_hbm, triangle_ref, projected_ref,
                 remainder_ref, panel, slab, total, inbox, work, ahead3, inverse, panel3, turned3, slab3,
                 upper3, upper_t3, inverse3, inverse_t3, projected3, both3, y3, last3,
                 l_sem, s_sem, a_recv, b_recv, r_send, r_recv):
    mesh_ids = pl.DeviceIdType.MESH
    mine = lax.axis_index("dev")
    rank = lax.axis_index("half") * groups + lax.axis_index("grp")
    pairs = devs // 2
    pair, parity = mine // 2, mine % 2
    levels = (halves * groups).bit_length() - 1
    blocks, size, _ = panel.shape
    rows = size // devs
    p = blocks * NB
    n = slab.shape[1]
    last = blocks - 1
    where, stretch, _ = packing(p, n)

    def slot(dev):
        return pl.ds(pl.multiple_of(dev * rows, rows), rows)

    def same(step):
        return ((pair + step) % pairs) * 2 + parity

    def at_rank(level):
        bit = 1 << level
        other = rank + bit * (1 - 2 * ((rank // bit) % 2))
        return {"half": other // groups, "grp": other % groups}

    def blk(i):
        return slice(i * NB, (i + 1) * NB)

    for j in range(blocks):
        pltpu.make_async_copy(panel_hbm.at[:, blk(j)], panel.at[j, slot(mine)], l_sem.at[0]).start()
    slab_load = pltpu.make_async_copy(trailing_hbm, slab, l_sem.at[1])
    slab_load.start()

    beside = pair * 2 + 1 - parity
    peers = [{"dev": same(step)} for step in range(1, pairs)] + [{"dev": beside}]
    peers += [at_rank(level) for level in range(levels)]
    barrier = pltpu.get_barrier_semaphore()
    for peer in peers:
        pl.semaphore_signal(barrier, inc=1, device_id=peer, device_id_type=mesh_ids)
    pl.semaphore_wait(barrier, len(peers))

    def arrival(j, step):
        return pltpu.make_async_remote_copy(
            src_ref=panel.at[j, slot(mine)], dst_ref=panel.at[j, slot(mine)],
            send_sem=s_sem.at[0], recv_sem=a_recv.at[j, step - 1],
            device_id={"dev": same(step)}, device_id_type=mesh_ids)

    def passing(j, step):
        owner = same(pairs - step)
        return pltpu.make_async_remote_copy(
            src_ref=panel.at[j, slot(owner)], dst_ref=panel.at[j, slot(owner)],
            send_sem=s_sem.at[1], recv_sem=b_recv.at[j],
            device_id={"dev": beside}, device_id_type=mesh_ids)

    def send(j):
        if j < blocks:
            for step in range(1, pairs):
                arrival(j, step).start()

    own = panel.at[:, slot(mine)]
    pltpu.make_async_copy(own, own, l_sem.at[0]).wait()
    send(0)
    passing(0, 0).start()

    def forward(j):
        near = jnp.minimum(pair, pairs - 1 - pair)
        far = jnp.where(pair < pairs - 1 - pair, 1, -1)
        for k in range(pairs - 1):
            offset = jnp.where(k < 2 * near, (k // 2 + 1) * (1 - 2 * (k % 2)), (k - near + 1) * far)
            step = (pairs - offset) % pairs
            arrival(j, step).wait_recv()
            passing(j, step).start()
            if j == 0 and k == 0:
                send(1)
        send(j + 2)
        if j + 1 < blocks:
            passing(j + 1, 0).start()

    names = list(stretch)

    def reduction(name, level):
        begin, count = stretch[name]
        which = names.index(name)
        half = count // 2
        low = begin + (rank % 2) * half
        keep = pl.ds(pl.multiple_of(low, 8), half)
        give = pl.ds(pl.multiple_of(2 * begin + half - low, 8), half)
        copy = pltpu.make_async_remote_copy(
            src_ref=total.at[keep if level else give],
            dst_ref=inbox.at[level, pl.ds(begin // 2, half)],
            send_sem=r_send.at[level, which], recv_sem=r_recv.at[level, which],
            device_id=at_rank(level if level < levels else 0), device_id_type=mesh_ids)
        return copy, keep, give, slice(begin // 2, begin // 2 + half)

    def together(part, which, at):
        return pltpu.make_async_remote_copy(
            src_ref=part, dst_ref=part, send_sem=s_sem.at[which], recv_sem=b_recv.at[at],
            device_id={"dev": beside}, device_id_type=mesh_ids)

    def arrive(j):
        together(panel.at[j, pl.ds(0, pairs * rows)], 1, j).wait_recv()

    def prepare(j):
        x = panel[j]
        for s, part in enumerate(split(x)):
            panel3[s, j] = part
        for s, part in enumerate(split(x.T)):
            turned3[s, blk(j), :] = part

    def products(j):
        right = [jnp.concatenate([*(panel3[s, i] for i in range(j + 1)), slab3[s]], axis=1)
                 for s in range(3)]
        out = mm([turned3[s, blk(j), :] for s in range(3)], right)
        for i in range(j + 1):
            at = where["gram", i, j]
            total[at:at + NB, :] = out[:, blk(i)]
        for q in range(n // NB):
            at = where["cross", j, q]
            total[at:at + NB, :] = out[:, blk(j + 1 + q)]

    def begin(name):
        reduction(name, 0)[0].start()

    def receive(j):
        arrive(j)
        prepare(j)

    def load_slab():
        slab_load.wait()
        for s, part in enumerate(split(slab[...])):
            slab3[s] = part

    def advance(name, level):
        copy, keep, give, place = reduction(name, level)
        copy.wait()
        if level < levels:
            total[keep, :] += inbox[level, place]
            reduction(name, level + 1)[0].start()
        else:
            total[give, :] = inbox[level, place]
            ready.add(name)

    queue = []

    def add(place, task, *args):
        queue.append((place, functools.partial(task, *args)))

    for j in range(1, blocks):
        add(FORWARDS[min(j, 3)], forward, j)
    for name in names:
        kind, j = name
        start, *at = PLACES.get(name, ((48, 48), 49, 50, 51))
        if kind == "gram":
            add(start[0], receive, j)
            add(start[1], products, j)
        add(start[-1], begin, name)
        for level in range(levels + 1):
            add(at[0 if level == 0 else 2 if level == levels else 1], advance, name, level)
    ready = set()

    def pump(place):
        while queue and queue[0][0] <= place:
            queue.pop(0)[1]()

    def ensure(name):
        at = 0
        while name not in ready:
            while queue[at][1].func is need:
                at += 1
            queue.pop(at)[1]()

    def gram_of(i, j):
        at = where["gram", i, j]
        return total[at:at + NB, :]

    def cross_of(i):
        pieces = [where["cross", i, q] for q in range(n // NB)]
        return jnp.concatenate([total[at:at + NB, :] for at in pieces], axis=1)

    def put(ref, at, x):
        for s, part in enumerate(split(x)):
            ref[(s, *at)] = part

    def get(ref, *at):
        return [ref[(s, *at)] for s in range(3)]

    def lead(i, j):
        a = gram_of(i, j)
        if i:
            past = slice(0, i * NB)
            a = a - mm(get(upper_t3, blk(j), past), get(upper3, past, blk(i)))
        return a.T, a

    def link(i, j, a, turned):
        right = mm(get(inverse3, blk(i)), a)
        turned = mm_nt(turned, get(inverse3, blk(i)))
        triangle_ref[blk(i), blk(j)] = right
        put(upper3, (blk(i), blk(j)), right)
        put(upper_t3, (blk(j), blk(i)), turned)

    def early_link(i, j):
        a, turned = lead(i, j)
        link(i, j, split(a), split(turned))

    def early(j):
        i = j - 1
        a, turned = lead(i, j)
        put(ahead3, (0,), a)
        put(ahead3, (1,), turned)
        d = gram_of(j, j)
        if i:
            past = slice(0, i * NB)
            d = d - mm(get(upper_t3, blk(j), past), get(upper3, past, blk(j)))
        work[...] = d

    def late(j):
        i = j - 1
        link(i, j, get(ahead3, 0), get(ahead3, 1))
        work[...] -= mm(get(upper_t3, blk(j), blk(i)), get(upper3, blk(i), blk(j)))

    def projection(j):
        d = cross_of(j)
        if j:
            past = slice(0, j * NB)
            d = d - mm(get(upper_t3, blk(j), past), get(projected3, past))
        return d

    load_slab()
    forward(0)
    for i in range(1, blocks):
        triangle_ref[blk(i), 0:i * NB] = jnp.zeros((NB, i * NB), F32)

    def project(j):
        out = mm(get(inverse3, blk(j)), split(projection(j)))
        projected_ref[blk(j), :] = out
        put(projected3, (blk(j),), out)

    def solve_back(k):
        rhs = jnp.concatenate([projected_ref[blk(k), :], triangle_ref[blk(k), blk(last)]], axis=1)
        if k + 1 < last:
            after = slice((k + 1) * NB, last * NB)
            rhs = rhs - mm(get(upper3, blk(k), after), get(both3, after))
        put(both3, (blk(k),), mm(get(inverse_t3, blk(k)), split(rhs)))

    def reduce_rest(at):
        rest = jnp.concatenate([slab[at, :], panel[last, at, :]], axis=1)
        if last:
            before = [jnp.concatenate([panel3[s, k, at, :] for k in range(last)], axis=1)
                      for s in range(3)]
            rest = rest - mm(before, get(both3, slice(0, last * NB)))
        remainder_ref[at, :] = rest[:, 0:n]
        put(y3, (at,), rest[:, n:n + NB])

    def need(task, names, *args):
        for name in names:
            ensure(name)
        task(*args)

    for j in range(1, blocks):
        for i in range(j - 1):
            add(16 * j + (-3 if j == 2 else -8) + 3 * i, need, early_link, [("gram", j)], i, j)
        add(16 * j - 1.5, need, early, [("gram", j)], j)
        name = ("cross", max(j - 1, min(1, last)))
        add(16 * j + (8 if j == 1 else 3 if j < last else 1), need, project, [name], j - 1)
    add(16 * last + 1.5, need, lambda: put(last3, (), projection(last)), [("cross", last)])
    for k in range(last):
        add(16 * last + 2 + 2 * k, solve_back, last - 1 - k)
    for r in range(0, size, NB):
        add(16 * last + 4 + 2 * last + 2 * (r // NB), reduce_rest, slice(r, r + NB))
    queue.sort(key=lambda x: x[0])

    for j in range(blocks):
        ensure(("gram", j))
        if j:
            pump(16 * j - 1)
            late(j)
        else:
            work[...] = gram_of(0, 0)
        factor_block([work[SUB * g:SUB * (g + 1), :] for g in range(NB // SUB)],
                     triangle_ref, inverse, j * NB, j * NB, lambda b: pump(16 * j + b))
        done = inverse[blk(j), :]
        put(inverse3, (blk(j),), done)
        if j < last:
            put(inverse_t3, (blk(j),), done.T)
    while queue:
        queue.pop(0)[1]()
    out = mm(get(inverse3, blk(last)), get(last3))
    projected_ref[blk(last), :] = out
    basis = mm_nt(get(y3), get(inverse3, blk(last)))
    remainder_ref[...] = remainder_ref[...] - mm(split(basis), split(out))
    together(panel.at[:, pl.ds(0, (pairs - 1) * rows)], 0, 0).wait_send()
    together(panel.at[:, pl.ds(0, pairs * rows)], 1, 0).wait_send()


def on_device(mesh, panel_block, trailing):
    halves, groups, devs = (mesh.shape[name] for name in ("half", "grp", "dev"))
    rows, p = panel_block.shape
    size, n = trailing.shape
    blocks = p // NB
    _, stretch, length = packing(p, n)
    levels = (halves * groups).bit_length() - 1
    vmem, dma = pltpu.VMEM, pltpu.SemaphoreType.DMA
    space = pl.BlockSpec(memory_space=pl.ANY)
    inside = pl.BlockSpec(memory_space=pltpu.VMEM)
    return pl.pallas_call(
        functools.partial(fused_kernel, halves, groups, devs),
        out_shape=(
            pltpu.VMEM((p, p), F32),
            pltpu.VMEM((p, n), F32),
            pltpu.VMEM((size, n), F32),
        ),
        in_specs=[space] * 2,
        out_specs=(inside,) * 3,
        scratch_shapes=[
            vmem((blocks, size, NB), F32),
            vmem((size, n), F32),
            vmem((length, NB), F32),
            vmem((levels + 1, length // 2, NB), F32),
            vmem((NB, NB), F32),
            vmem((3, 2, NB, NB), BF16),
            vmem((p, NB), F32),
            vmem((3, blocks, size, NB), BF16),
            vmem((3, p, size), BF16),
            vmem((3, size, n), BF16),
            vmem((3, p, p), BF16),
            vmem((3, p, p), BF16),
            vmem((3, p, NB), BF16),
            vmem((3, p, NB), BF16),
            vmem((3, p, n), BF16),
            vmem((3, p, n + NB), BF16),
            vmem((3, size, NB), BF16),
            vmem((3, NB, n), BF16),
            dma((2,)), dma((2,)), dma((blocks, devs // 2 - 1)), dma((blocks,)),
            dma((levels + 1, len(stretch))), dma((levels + 1, len(stretch))),
        ],
        compiler_params=pltpu.CompilerParams(collective_id=0, has_side_effects=True),
        name="factor_project",
    )(panel_block, trailing)


def solution(mesh):
    placed = (P(("half", "grp", "dev"), None), P(("half", "grp"), "dev"))
    return jax.shard_map(
        functools.partial(on_device, mesh),
        mesh=mesh,
        in_specs=placed,
        out_specs=(P(), P(None, "dev"), P(("half", "grp"), "dev")),
        check_vma=False,
    )
```

```python
import functools

import jax
import jax.numpy as jnp
from jax import lax
from jax.experimental import pallas as pl
from jax.experimental.pallas import tpu as pltpu
from jax.sharding import PartitionSpec as P

NB = 128
SUB = 8
LIMIT = 24 << 20
PAIR = 2
F32 = jnp.float32
BF16 = jnp.bfloat16
LEFT = (0, 0, 1, 0, 1, 2)
RIGHT = (0, 1, 0, 2, 1, 0)


PLACES = {
    ("gram", 0): ((-12, -12), -10, -7, -5),
    ("gram", 1): ((-6, -6), 2, 15, 15.9),
    ("cross", 1): ((2.1,), 9, 19, 23),
    ("gram", 2): ((6, 7), 13, 24, 28),
    ("gram", 3): ((14.5, 15.2), 18, 35, 39.5),
    ("cross", 2): ((20,), 25, 40, 43),
    ("cross", 3): ((21,), 28.5, 44, 47.9),
}

FORWARDS = (0, -11, -9, 0)


def split(x):
    high = x.astype(BF16)
    rest = x - high.astype(F32)
    middle = rest.astype(BF16)
    low = (rest - middle.astype(F32)).astype(BF16)
    return high, middle, low


def wide(parts, which, axis):
    return jnp.concatenate([parts[s] for s in which], axis=axis)


def contract(a, b, dim):
    return lax.dot_general(a, b, (((1,), (dim,)), ((), ())), preferred_element_type=F32)


def mm(a, b):
    return contract(wide(a, LEFT, 1), wide(b, RIGHT, 0), 0)


def mm_nt(a, b):
    return contract(wide(a, LEFT, 1), wide(b, RIGHT, 1), 1)


def blk(i):
    return slice(i * NB, (i + 1) * NB)


def put(ref, at, x):
    for s, part in enumerate(split(x)):
        ref[(s, *at)] = part


def get(ref, *at):
    return [ref[(s, *at)] for s in range(3)]


def lanes_of(x, at):
    return jnp.take_along_axis(x, jnp.full(x.shape, at, jnp.int32), axis=1)


def factor_block(block, upper_ref, inverse_ref, row0, col0, hook):
    tile = (SUB, NB)
    lane = lax.broadcasted_iota(jnp.int32, tile, 1)
    row = lax.broadcasted_iota(jnp.int32, tile, 0)
    here = [row == j for j in range(SUB)]
    block = list(block)
    groups = len(block)
    ups, lows = [], []
    following = None

    def one(x, at):
        return jnp.broadcast_to(x[at:at + 1, :], tile)

    for b in range(groups):
        hook(b)
        c0 = SUB * b
        own = block[b]
        near = min(groups, (b // PAIR + 2) * PAIR)
        inside = (lane >= c0) & (lane < c0 + SUB)
        opens = b % PAIR == 0
        cols = [lanes_of(own, c0 + t) for t in range(SUB)] if opens else following
        columns = {g: [lanes_of(block[g], c0 + t) for t in range(SUB)] for g in range(b + 1, near)}
        if opens:
            following = [lanes_of(block[b + 1], c0 + SUB + t) for t in range(SUB)]
            below = list(columns[b + 1])
        v = jnp.where(inside, jnp.where(lane == row + c0, 1.0, 0.0), own)
        w = own
        up = low = None
        raw = list(cols)
        for j in range(SUB):
            top = [one(raw[t], j) if t >= j else None for t in range(SUB)]
            rs = lax.rsqrt(top[j])
            r = rs * rs
            e = cols[j] * r
            vj, wj = one(v, j), one(w, j)
            vs, ws = vj * rs, wj * rs
            up = ws if j == 0 else jnp.where(here[j], ws, up)
            low = vs if j == 0 else jnp.where(here[j], vs, low)
            v = jnp.where(here[j], vj * r, v - e * vj)
            if j + 1 < SUB:
                w = w - e * wj
            for t in range(j + 1, SUB):
                raw[t] = cols[t] - (cols[j] * top[t]) * r
                cols[t] = jnp.where(here[j], top[t] * r, raw[t])
            if opens:
                share = below[j] * r
                for t in range(SUB):
                    following[t] = following[t] - share * one(below[j], t)
                for t in range(j + 1, SUB):
                    below[t] = below[t] - (below[j] * top[t]) * r
        up = jnp.where(lane >= row + c0, up, 0.0)
        low = jnp.where(lane <= row + c0, low, 0.0)
        upper_ref[row0 + c0:row0 + c0 + SUB, col0:col0 + NB] = up
        inverse_ref[row0 + c0:row0 + c0 + SUB, :] = low
        ups.append(up)
        lows.append(low)
        if b + 1 < near:
            vt = [one(v, t) for t in range(SUB)]
        for g in range(b + 1, near):
            terms = [columns[g][t] * vt[t] for t in range(SUB)]
            while len(terms) > 1:
                terms = [terms[i] + terms[i + 1] for i in range(0, len(terms), 2)]
            block[g] = jnp.where(inside, 0.0, block[g]) - terms[0]
        if not opens and near < groups:
            end = c0 + SUB
            past = lane >= end
            us = jnp.concatenate([jnp.where(past, u, 0.0) for u in ups[-PAIR:]], axis=0)
            vs = jnp.concatenate(
                [jnp.where(past, u, x) for u, x in zip(ups[-PAIR:], lows[-PAIR:])], axis=0)
            res = lax.dot_general(
                wide(split(us), LEFT, 0), wide(split(vs), RIGHT, 0), (((0,), (0,)), ((), ())),
                preferred_element_type=F32)
            done = (lane >= end - PAIR * SUB) & (lane < end)
            for g in range(near, groups):
                block[g] = jnp.where(done, 0.0, block[g]) - res[SUB * g:SUB * (g + 1), :]


def packing(p, n):
    blocks = p // NB
    regions = [("gram", (0,))]
    for j in range(1, blocks):
        regions.append(("gram", (j,)))
        regions.append(("cross", (0, 1) if j == 1 else (j,)))
    if blocks == 1:
        regions.append(("cross", (0,)))
    where, stretch = {}, {}
    at = 0
    for kind, members in regions:
        first = at
        for j in members:
            for i in range(j + 1 if kind == "gram" else n // NB):
                where[(kind, i, j) if kind == "gram" else (kind, j, i)] = at
                at += NB
        stretch[kind, members[-1]] = (first, at - first)
    return where, stretch, at


def lead_kernel(halves, groups, devs, panel_hbm, trailing_hbm, triangle_ref, projected_ref, work,
                total, panel, panel3, slab, upper3, upper_t3, inverse3, inverse_t3, projected3,
                inbox, ahead3, inverse, turned3, slab3, l_sem, s_sem, a_recv, b_recv, r_send, r_recv):
    mesh_ids = pl.DeviceIdType.MESH
    mine = lax.axis_index("dev")
    rank = lax.axis_index("half") * groups + lax.axis_index("grp")
    pairs = devs // 2
    pair, parity = mine // 2, mine % 2
    levels = (halves * groups).bit_length() - 1
    blocks, size, _ = panel.shape
    rows = size // devs
    p = blocks * NB
    n = slab.shape[1]
    last = blocks - 1
    where, stretch, _ = packing(p, n)

    def slot(dev):
        return pl.ds(pl.multiple_of(dev * rows, rows), rows)

    def same(step):
        return ((pair + step) % pairs) * 2 + parity

    def at_rank(level):
        bit = 1 << level
        other = rank + bit * (1 - 2 * ((rank // bit) % 2))
        return {"half": other // groups, "grp": other % groups}

    for j in range(blocks):
        pltpu.make_async_copy(panel_hbm.at[:, blk(j)], panel.at[j, slot(mine)], l_sem.at[0]).start()
    slab_load = pltpu.make_async_copy(trailing_hbm, slab, l_sem.at[1])
    slab_load.start()

    beside = pair * 2 + 1 - parity
    peers = [{"dev": same(step)} for step in range(1, pairs)] + [{"dev": beside}]
    peers += [at_rank(level) for level in range(levels)]
    barrier = pltpu.get_barrier_semaphore()
    for peer in peers:
        pl.semaphore_signal(barrier, inc=1, device_id=peer, device_id_type=mesh_ids)
    pl.semaphore_wait(barrier, len(peers))

    def arrival(j, step):
        return pltpu.make_async_remote_copy(
            src_ref=panel.at[j, slot(mine)], dst_ref=panel.at[j, slot(mine)],
            send_sem=s_sem.at[0], recv_sem=a_recv.at[j, step - 1],
            device_id={"dev": same(step)}, device_id_type=mesh_ids)

    def passing(j, step):
        owner = same(pairs - step)
        return pltpu.make_async_remote_copy(
            src_ref=panel.at[j, slot(owner)], dst_ref=panel.at[j, slot(owner)],
            send_sem=s_sem.at[1], recv_sem=b_recv.at[j],
            device_id={"dev": beside}, device_id_type=mesh_ids)

    def send(j):
        if j < blocks:
            for step in range(1, pairs):
                arrival(j, step).start()

    own = panel.at[:, slot(mine)]
    pltpu.make_async_copy(own, own, l_sem.at[0]).wait()
    send(0)
    passing(0, 0).start()

    def forward(j):
        near = jnp.minimum(pair, pairs - 1 - pair)
        far = jnp.where(pair < pairs - 1 - pair, 1, -1)
        for k in range(pairs - 1):
            offset = jnp.where(k < 2 * near, (k // 2 + 1) * (1 - 2 * (k % 2)), (k - near + 1) * far)
            step = (pairs - offset) % pairs
            arrival(j, step).wait_recv()
            passing(j, step).start()
            if j == 0 and k == 0:
                send(1)
        send(j + 2)
        if j + 1 < blocks:
            passing(j + 1, 0).start()

    names = list(stretch)

    def reduction(name, level):
        begin, count = stretch[name]
        which = names.index(name)
        half = count // 2
        low = begin + (rank % 2) * half
        keep = pl.ds(pl.multiple_of(low, 8), half)
        give = pl.ds(pl.multiple_of(2 * begin + half - low, 8), half)
        copy = pltpu.make_async_remote_copy(
            src_ref=total.at[keep if level else give],
            dst_ref=inbox.at[level, pl.ds(begin // 2, half)],
            send_sem=r_send.at[level, which], recv_sem=r_recv.at[level, which],
            device_id=at_rank(level if level < levels else 0), device_id_type=mesh_ids)
        return copy, keep, give, slice(begin // 2, begin // 2 + half)

    def together(part, which, at):
        return pltpu.make_async_remote_copy(
            src_ref=part, dst_ref=part, send_sem=s_sem.at[which], recv_sem=b_recv.at[at],
            device_id={"dev": beside}, device_id_type=mesh_ids)

    def arrive(j):
        together(panel.at[j, pl.ds(0, pairs * rows)], 1, j).wait_recv()

    def prepare(j):
        x = panel[j]
        for s, part in enumerate(split(x)):
            panel3[s, j] = part
        for s, part in enumerate(split(x.T)):
            turned3[s, blk(j), :] = part

    def products(j):
        right = [jnp.concatenate([*(panel3[s, i] for i in range(j + 1)), slab3[s]], axis=1)
                 for s in range(3)]
        out = mm([turned3[s, blk(j), :] for s in range(3)], right)
        for i in range(j + 1):
            at = where["gram", i, j]
            total[at:at + NB, :] = out[:, blk(i)]
        for q in range(n // NB):
            at = where["cross", j, q]
            total[at:at + NB, :] = out[:, blk(j + 1 + q)]

    def begin(name):
        reduction(name, 0)[0].start()

    def receive(j):
        arrive(j)
        prepare(j)

    def load_slab():
        slab_load.wait()
        for s, part in enumerate(split(slab[...])):
            slab3[s] = part

    def advance(name, level):
        copy, keep, give, place = reduction(name, level)
        copy.wait()
        if level < levels:
            total[keep, :] += inbox[level, place]
            reduction(name, level + 1)[0].start()
        else:
            total[give, :] = inbox[level, place]
            ready.add(name)

    queue = []

    def add(place, task, *args):
        queue.append((place, functools.partial(task, *args)))

    for j in range(1, blocks):
        add(FORWARDS[min(j, 3)], forward, j)
    for name in names:
        kind, j = name
        start, *at = PLACES.get(name, ((48, 48), 49, 50, 51))
        if kind == "gram":
            add(start[0], receive, j)
            add(start[1], products, j)
        add(start[-1], begin, name)
        for level in range(levels + 1):
            add(at[0 if level == 0 else 2 if level == levels else 1], advance, name, level)
    ready = set()

    def pump(place):
        while queue and queue[0][0] <= place:
            queue.pop(0)[1]()

    def ensure(name):
        at = 0
        while name not in ready:
            while queue[at][1].func is need:
                at += 1
            queue.pop(at)[1]()

    def gram_of(i, j):
        at = where["gram", i, j]
        return total[at:at + NB, :]

    def cross_of(i):
        pieces = [where["cross", i, q] for q in range(n // NB)]
        return jnp.concatenate([total[at:at + NB, :] for at in pieces], axis=1)

    def lead(i, j):
        a = gram_of(i, j)
        if i:
            past = slice(0, i * NB)
            a = a - mm(get(upper_t3, blk(j), past), get(upper3, past, blk(i)))
        return a.T, a

    def link(i, j, a, turned):
        right = mm(get(inverse3, blk(i)), a)
        turned = mm_nt(turned, get(inverse3, blk(i)))
        triangle_ref[blk(i), blk(j)] = right
        put(upper3, (blk(i), blk(j)), right)
        put(upper_t3, (blk(j), blk(i)), turned)

    def early_link(i, j):
        a, turned = lead(i, j)
        link(i, j, split(a), split(turned))

    def early(j):
        i = j - 1
        a, turned = lead(i, j)
        put(ahead3, (0,), a)
        put(ahead3, (1,), turned)
        d = gram_of(j, j)
        if i:
            past = slice(0, i * NB)
            d = d - mm(get(upper_t3, blk(j), past), get(upper3, past, blk(j)))
        work[...] = d

    def late(j):
        i = j - 1
        link(i, j, get(ahead3, 0), get(ahead3, 1))
        work[...] -= mm(get(upper_t3, blk(j), blk(i)), get(upper3, blk(i), blk(j)))

    def projection(j):
        d = cross_of(j)
        if j:
            past = slice(0, j * NB)
            d = d - mm(get(upper_t3, blk(j), past), get(projected3, past))
        return d

    load_slab()
    forward(0)
    for i in range(1, blocks):
        triangle_ref[blk(i), 0:i * NB] = jnp.zeros((NB, i * NB), F32)

    def project(j):
        out = mm(get(inverse3, blk(j)), split(projection(j)))
        projected_ref[blk(j), :] = out
        put(projected3, (blk(j),), out)

    def need(task, names, *args):
        for name in names:
            ensure(name)
        task(*args)

    for j in range(1, blocks):
        for i in range(j - 1):
            add(16 * j + (-3 if j == 2 else -8) + 3 * i, need, early_link, [("gram", j)], i, j)
        add(16 * j - 1.5, need, early, [("gram", j)], j)
        if j < last:
            add(16 * j + (8 if j == 1 else 3), need, project, [("cross", max(j - 1, 1))], j - 1)
    queue.sort(key=lambda x: x[0])

    for j in range(blocks):
        ensure(("gram", j))
        if j:
            pump(16 * j - 1)
            late(j)
        else:
            work[...] = gram_of(0, 0)
        if j < last:
            factor_block([work[SUB * g:SUB * (g + 1), :] for g in range(NB // SUB)],
                         triangle_ref, inverse, j * NB, j * NB, lambda b: pump(16 * j + b))
            done = inverse[blk(j), :]
            put(inverse3, (blk(j),), done)
            put(inverse_t3, (blk(j),), done.T)
    while queue:
        queue.pop(0)[1]()
    together(panel.at[:, pl.ds(0, (pairs - 1) * rows)], 0, 0).wait_send()
    together(panel.at[:, pl.ds(0, pairs * rows)], 1, 0).wait_send()


def last_kernel(triangle_in, projected_in, work, total, panel, panel3, slab, upper3, upper_t3,
                inverse3, inverse_t3, projected3, triangle_ref, projected_ref, remainder_ref,
                corner, inverse, projected, remainder, fresh3, both3, y3, last3, sems):
    blocks, size, _ = panel.shape
    n = slab.shape[1]
    last = blocks - 1
    where, _, _ = packing(blocks * NB, n)
    copies = []

    def send(source, target):
        copies.append(pltpu.make_async_copy(source, target, sems.at[len(copies)]))
        copies[-1].start()

    send(triangle_in.at[0:last * NB], triangle_ref.at[0:last * NB])
    send(triangle_in.at[blk(last), 0:last * NB], triangle_ref.at[blk(last), 0:last * NB])
    if last > 1:
        send(projected_in.at[0:(last - 1) * NB], projected_ref.at[0:(last - 1) * NB])

    def projection(j, before):
        pieces = [where["cross", j, q] for q in range(n // NB)]
        d = jnp.concatenate([total[at:at + NB, :] for at in pieces], axis=1)
        return d - mm(get(upper_t3, blk(j), slice(0, j * NB)), before) if j else d

    def project():
        j = last - 1
        out = mm(get(inverse3, blk(j)), split(projection(j, get(projected3, slice(0, j * NB)))))
        projected[blk(j), :] = out
        put(fresh3, (), out)
        send(projected.at[blk(j)], projected_ref.at[blk(j)])

    def project_last():
        j = last - 1
        before = [jnp.concatenate([projected3[s, 0:j * NB], fresh3[s]], axis=0) if j else fresh3[s]
                  for s in range(3)]
        put(last3, (), projection(last, before))

    def solve_back(k):
        own = projected if k == last - 1 else projected_in
        rhs = jnp.concatenate([own[blk(k), :], triangle_in[blk(k), blk(last)]], axis=1)
        if k + 1 < last:
            after = slice((k + 1) * NB, last * NB)
            rhs = rhs - mm(get(upper3, blk(k), after), get(both3, after))
        put(both3, (blk(k),), mm(get(inverse_t3, blk(k)), split(rhs)))

    def reduce_rest(at):
        rest = jnp.concatenate([slab[at, :], panel[last, at, :]], axis=1)
        if last:
            before = [jnp.concatenate([panel3[s, k, at, :] for k in range(last)], axis=1)
                      for s in range(3)]
            rest = rest - mm(before, get(both3, slice(0, last * NB)))
        remainder[at, :] = rest[:, 0:n]
        put(y3, (at,), rest[:, n:n + NB])

    tasks = {}
    if last:
        tasks[1] = [project, project_last]
    for k in range(last):
        tasks.setdefault(2 + 2 * k, []).append(functools.partial(solve_back, last - 1 - k))
    for r in range(0, size, NB):
        tasks.setdefault(min(4 + 2 * last + 2 * (r // NB), 15), []).append(
            functools.partial(reduce_rest, slice(r, r + NB)))
    if not last:
        put(last3, (), projection(0, None))

    def hook(b):
        for task in tasks.get(b, []):
            task()

    factor_block([work[SUB * g:SUB * (g + 1), :] for g in range(NB // SUB)], corner, inverse, 0, 0, hook)
    send(corner, triangle_ref.at[blk(last), blk(last)])
    done = split(inverse[...])
    out = mm(done, get(last3))
    projected[blk(last), :] = out
    send(projected.at[blk(last)], projected_ref.at[blk(last)])
    basis = mm_nt(get(y3), done)
    remainder[...] = remainder[...] - mm(split(basis), split(out))
    send(remainder, remainder_ref)
    for copy in copies:
        copy.wait()


def on_device(mesh, panel_block, trailing):
    halves, groups, devs = (mesh.shape[name] for name in ("half", "grp", "dev"))
    rows, p = panel_block.shape
    size, n = trailing.shape
    blocks = p // NB
    _, stretch, length = packing(p, n)
    levels = (halves * groups).bit_length() - 1
    vmem, dma = pltpu.VMEM, pltpu.SemaphoreType.DMA
    space = pl.BlockSpec(memory_space=pl.ANY)
    inside = pl.BlockSpec(memory_space=pltpu.VMEM)
    kept = (
        vmem((p, p), F32), vmem((p, n), F32), vmem((NB, NB), F32), vmem((length, NB), F32),
        vmem((blocks, size, NB), F32), vmem((3, blocks, size, NB), BF16), vmem((size, n), F32),
        vmem((3, p, p), BF16), vmem((3, p, p), BF16), vmem((3, p, NB), BF16), vmem((3, p, NB), BF16),
        vmem((3, p, n), BF16),
    )
    found = pl.pallas_call(
        functools.partial(lead_kernel, halves, groups, devs),
        out_shape=kept,
        in_specs=[space] * 2,
        out_specs=(inside,) * len(kept),
        scratch_shapes=[
            vmem((levels + 1, length // 2, NB), F32),
            vmem((3, 2, NB, NB), BF16),
            vmem((p, NB), F32),
            vmem((3, p, size), BF16),
            vmem((3, size, n), BF16),
            dma((2,)), dma((2,)), dma((blocks, devs // 2 - 1)), dma((blocks,)),
            dma((levels + 1, len(stretch))), dma((levels + 1, len(stretch))),
        ],
        compiler_params=pltpu.CompilerParams(
            collective_id=0, has_side_effects=True, vmem_limit_bytes=LIMIT),
        name="lead_blocks",
    )(*(pltpu.with_memory_space_constraint(x, pltpu.HBM) for x in (panel_block, trailing)))
    return pl.pallas_call(
        last_kernel,
        out_shape=(
            jax.ShapeDtypeStruct((p, p), F32),
            jax.ShapeDtypeStruct((p, n), F32),
            jax.ShapeDtypeStruct((size, n), F32),
        ),
        in_specs=[inside] * len(kept),
        out_specs=(space,) * 3,
        scratch_shapes=[
            vmem((NB, NB), F32), vmem((NB, NB), F32), vmem((p, n), F32), vmem((size, n), F32),
            vmem((3, NB, n), BF16), vmem((3, p, n + NB), BF16), vmem((3, size, NB), BF16),
            vmem((3, NB, n), BF16), dma((7,)),
        ],
        compiler_params=pltpu.CompilerParams(vmem_limit_bytes=LIMIT),
        name="last_block",
    )(*(pltpu.with_memory_space_constraint(x, pltpu.VMEM) for x in found))


def solution(mesh):
    placed = (P(("half", "grp", "dev"), None), P(("half", "grp"), "dev"))
    return jax.shard_map(
        functools.partial(on_device, mesh),
        mesh=mesh,
        in_specs=placed,
        out_specs=(P(), P(None, "dev"), P(("half", "grp"), "dev")),
        check_vma=False,
    )
```

```python
import functools

import jax
import jax.numpy as jnp
from jax import lax
from jax.experimental import pallas as pl
from jax.experimental.pallas import tpu as pltpu
from jax.sharding import PartitionSpec as P

NB = 128
SUB = 8
LIMIT = 24 << 20
PAIR = 2
F32 = jnp.float32
BF16 = jnp.bfloat16
LEFT = (0, 0, 1, 0, 1, 2)
RIGHT = (0, 1, 0, 2, 1, 0)


PLACES = {
    ("gram", 0): ((-12, -12), -10, -7, -5),
    ("gram", 1): ((-6, -6), 2, 15.3, 15.9),
    ("cross", 1): ((2.1,), 9, 22, 30),
    ("gram", 2): ((6, 7), 13, 22.1, 28),
    ("gram", 3): ((15, 15.4), 18, 38, 43),
    ("cross", 2): ((20,), 31.2, 43.1, 47),
    ("cross", 3): ((21,), 31.3, 43.2, 47.1),
}

FORWARDS = (0, -11, -9, 0)


def split(x):
    high = x.astype(BF16)
    rest = x - high.astype(F32)
    middle = rest.astype(BF16)
    low = (rest - middle.astype(F32)).astype(BF16)
    return high, middle, low


def wide(parts, which, axis):
    return jnp.concatenate([parts[s] for s in which], axis=axis)


def contract(a, b, dim):
    return lax.dot_general(a, b, (((1,), (dim,)), ((), ())), preferred_element_type=F32)


def mm(a, b):
    return contract(wide(a, LEFT, 1), wide(b, RIGHT, 0), 0)


def mm_nt(a, b):
    return contract(wide(a, LEFT, 1), wide(b, RIGHT, 1), 1)


def blk(i):
    return slice(i * NB, (i + 1) * NB)


def put(ref, at, x):
    for s, part in enumerate(split(x)):
        ref[(s, *at)] = part


def get(ref, *at):
    return [ref[(s, *at)] for s in range(3)]


def lanes_of(x, at):
    return jnp.take_along_axis(x, jnp.full(x.shape, at, jnp.int32), axis=1)


def factor_block(block, upper_ref, inverse_ref, row0, col0, hook):
    tile = (SUB, NB)
    lane = lax.broadcasted_iota(jnp.int32, tile, 1)
    row = lax.broadcasted_iota(jnp.int32, tile, 0)
    here = [row == j for j in range(SUB)]
    block = list(block)
    groups = len(block)
    ups, lows = [], []
    following = None

    def one(x, at):
        return jnp.broadcast_to(x[at:at + 1, :], tile)

    for b in range(groups):
        hook(b)
        c0 = SUB * b
        own = block[b]
        near = min(groups, (b // PAIR + 2) * PAIR)
        inside = (lane >= c0) & (lane < c0 + SUB)
        opens = b % PAIR == 0
        cols = [lanes_of(own, c0 + t) for t in range(SUB)] if opens else following
        columns = {g: [lanes_of(block[g], c0 + t) for t in range(SUB)] for g in range(b + 1, near)}
        if opens:
            following = [lanes_of(block[b + 1], c0 + SUB + t) for t in range(SUB)]
            below = list(columns[b + 1])
        v = jnp.where(inside, jnp.where(lane == row + c0, 1.0, 0.0), own)
        w = own
        up = low = None
        raw = list(cols)
        for j in range(SUB):
            top = [one(raw[t], j) if t >= j else None for t in range(SUB)]
            rs = lax.rsqrt(top[j])
            r = rs * rs
            e = cols[j] * r
            vj, wj = one(v, j), one(w, j)
            vs, ws = vj * rs, wj * rs
            up = ws if j == 0 else jnp.where(here[j], ws, up)
            low = vs if j == 0 else jnp.where(here[j], vs, low)
            v = jnp.where(here[j], vj * r, v - e * vj)
            if j + 1 < SUB:
                w = w - e * wj
            for t in range(j + 1, SUB):
                raw[t] = cols[t] - (cols[j] * top[t]) * r
                cols[t] = jnp.where(here[j], top[t] * r, raw[t])
            if opens:
                share = below[j] * r
                for t in range(SUB):
                    following[t] = following[t] - share * one(below[j], t)
                for t in range(j + 1, SUB):
                    below[t] = below[t] - (below[j] * top[t]) * r
        up = jnp.where(lane >= row + c0, up, 0.0)
        low = jnp.where(lane <= row + c0, low, 0.0)
        upper_ref[row0 + c0:row0 + c0 + SUB, col0:col0 + NB] = up
        inverse_ref[row0 + c0:row0 + c0 + SUB, :] = low
        ups.append(up)
        lows.append(low)
        if b + 1 < near:
            vt = [one(v, t) for t in range(SUB)]
        for g in range(b + 1, near):
            terms = [columns[g][t] * vt[t] for t in range(SUB)]
            while len(terms) > 1:
                terms = [terms[i] + terms[i + 1] for i in range(0, len(terms), 2)]
            block[g] = jnp.where(inside, 0.0, block[g]) - terms[0]
        if not opens and near < groups:
            end = c0 + SUB
            past = lane >= end
            us = jnp.concatenate([jnp.where(past, u, 0.0) for u in ups[-PAIR:]], axis=0)
            vs = jnp.concatenate(
                [jnp.where(past, u, x) for u, x in zip(ups[-PAIR:], lows[-PAIR:])], axis=0)
            res = lax.dot_general(
                wide(split(us), LEFT, 0), wide(split(vs), RIGHT, 0), (((0,), (0,)), ((), ())),
                preferred_element_type=F32)
            done = (lane >= end - PAIR * SUB) & (lane < end)
            for g in range(near, groups):
                block[g] = jnp.where(done, 0.0, block[g]) - res[SUB * g:SUB * (g + 1), :]


def packing(p, n):
    blocks = p // NB
    regions = [("gram", (0,))]
    for j in range(1, blocks):
        regions.append(("gram", (j,)))
        regions.append(("cross", (0, 1) if j == 1 else (j,)))
    if blocks == 1:
        regions.append(("cross", (0,)))
    where, stretch = {}, {}
    at = 0
    for kind, members in regions:
        first = at
        for j in members:
            for i in range(j + 1 if kind == "gram" else n // NB):
                where[(kind, i, j) if kind == "gram" else (kind, j, i)] = at
                at += NB
        stretch[kind, members[-1]] = (first, at - first)
    return where, stretch, at


def lead_kernel(halves, groups, devs, panel_hbm, trailing_hbm, triangle_ref, projected_ref, work,
                total, panel, panel3, slab, upper3, upper_t3, inverse3, inverse_t3, projected3,
                inbox, ahead3, inverse, turned3, slab3, l_sem, s_sem, a_recv, b_recv, r_send, r_recv):
    mesh_ids = pl.DeviceIdType.MESH
    mine = lax.axis_index("dev")
    rank = lax.axis_index("half") * groups + lax.axis_index("grp")
    pairs = devs // 2
    pair, parity = mine // 2, mine % 2
    levels = (halves * groups).bit_length() - 1
    blocks, size, _ = panel.shape
    rows = size // devs
    p = blocks * NB
    n = slab.shape[1]
    last = blocks - 1
    where, stretch, _ = packing(p, n)

    def slot(dev):
        return pl.ds(pl.multiple_of(dev * rows, rows), rows)

    def same(step):
        return ((pair + step) % pairs) * 2 + parity

    def at_rank(level):
        bit = 1 << level
        other = rank + bit * (1 - 2 * ((rank // bit) % 2))
        return {"half": other // groups, "grp": other % groups}

    for j in range(blocks):
        pltpu.make_async_copy(panel_hbm.at[:, blk(j)], panel.at[j, slot(mine)], l_sem.at[0]).start()
    slab_load = pltpu.make_async_copy(trailing_hbm, slab, l_sem.at[1])
    slab_load.start()

    beside = pair * 2 + 1 - parity
    peers = [{"dev": same(step)} for step in range(1, pairs)] + [{"dev": beside}]
    peers += [at_rank(level) for level in range(levels)]
    barrier = pltpu.get_barrier_semaphore()
    for peer in peers:
        pl.semaphore_signal(barrier, inc=1, device_id=peer, device_id_type=mesh_ids)
    pl.semaphore_wait(barrier, len(peers))

    def arrival(j, step):
        return pltpu.make_async_remote_copy(
            src_ref=panel.at[j, slot(mine)], dst_ref=panel.at[j, slot(mine)],
            send_sem=s_sem.at[0], recv_sem=a_recv.at[j, step - 1],
            device_id={"dev": same(step)}, device_id_type=mesh_ids)

    def passing(j, step):
        owner = same(pairs - step)
        return pltpu.make_async_remote_copy(
            src_ref=panel.at[j, slot(owner)], dst_ref=panel.at[j, slot(owner)],
            send_sem=s_sem.at[1], recv_sem=b_recv.at[j],
            device_id={"dev": beside}, device_id_type=mesh_ids)

    def send(j):
        if j < blocks:
            for step in range(1, pairs):
                arrival(j, step).start()

    own = panel.at[:, slot(mine)]
    pltpu.make_async_copy(own, own, l_sem.at[0]).wait()
    send(0)
    passing(0, 0).start()

    def forward(j):
        near = jnp.minimum(pair, pairs - 1 - pair)
        far = jnp.where(pair < pairs - 1 - pair, 1, -1)
        for k in range(pairs - 1):
            offset = jnp.where(k < 2 * near, (k // 2 + 1) * (1 - 2 * (k % 2)), (k - near + 1) * far)
            step = (pairs - offset) % pairs
            arrival(j, step).wait_recv()
            passing(j, step).start()
            if j == 0 and k == 0:
                send(1)
        send(j + 2)
        if j + 1 < blocks:
            passing(j + 1, 0).start()

    names = list(stretch)

    def reduction(name, level):
        begin, count = stretch[name]
        which = names.index(name)
        half = count // 2
        low = begin + (rank % 2) * half
        keep = pl.ds(pl.multiple_of(low, 8), half)
        give = pl.ds(pl.multiple_of(2 * begin + half - low, 8), half)
        copy = pltpu.make_async_remote_copy(
            src_ref=total.at[keep if level else give],
            dst_ref=inbox.at[level, pl.ds(begin // 2, half)],
            send_sem=r_send.at[level, which], recv_sem=r_recv.at[level, which],
            device_id=at_rank(level if level < levels else 0), device_id_type=mesh_ids)
        return copy, keep, give, slice(begin // 2, begin // 2 + half)

    def together(part, which, at):
        return pltpu.make_async_remote_copy(
            src_ref=part, dst_ref=part, send_sem=s_sem.at[which], recv_sem=b_recv.at[at],
            device_id={"dev": beside}, device_id_type=mesh_ids)

    def arrive(j):
        together(panel.at[j, pl.ds(0, pairs * rows)], 1, j).wait_recv()

    def prepare(j):
        x = panel[j]
        for s, part in enumerate(split(x)):
            panel3[s, j] = part
        for s, part in enumerate(split(x.T)):
            turned3[s, blk(j), :] = part

    def products(j):
        right = [jnp.concatenate([*(panel3[s, i] for i in range(j + 1)), slab3[s]], axis=1)
                 for s in range(3)]
        out = mm([turned3[s, blk(j), :] for s in range(3)], right)
        for i in range(j + 1):
            at = where["gram", i, j]
            total[at:at + NB, :] = out[:, blk(i)]
        for q in range(n // NB):
            at = where["cross", j, q]
            total[at:at + NB, :] = out[:, blk(j + 1 + q)]

    def begin(name):
        reduction(name, 0)[0].start()

    def receive(j):
        arrive(j)
        prepare(j)

    def load_slab():
        slab_load.wait()
        for s, part in enumerate(split(slab[...])):
            slab3[s] = part

    def advance(name, level):
        copy, keep, give, place = reduction(name, level)
        copy.wait()
        if level < levels:
            total[keep, :] += inbox[level, place]
            reduction(name, level + 1)[0].start()
        else:
            total[give, :] = inbox[level, place]
            ready.add(name)

    queue = []

    def add(place, task, *args):
        queue.append((place, functools.partial(task, *args)))

    for j in range(1, blocks):
        add(FORWARDS[min(j, 3)], forward, j)
    for name in names:
        kind, j = name
        start, *at = PLACES.get(name, ((48, 48), 49, 50, 51))
        if kind == "gram":
            add(start[0], receive, j)
            add(start[1], products, j)
        add(start[-1], begin, name)
        for level in range(levels + 1):
            add(at[0 if level == 0 else 2 if level == levels else 1], advance, name, level)
    ready = set()

    def pump(place):
        while queue and queue[0][0] <= place:
            queue.pop(0)[1]()

    def ensure(name):
        at = 0
        while name not in ready:
            while queue[at][1].func is need:
                at += 1
            queue.pop(at)[1]()

    def gram_of(i, j):
        at = where["gram", i, j]
        return total[at:at + NB, :]

    def cross_of(i):
        pieces = [where["cross", i, q] for q in range(n // NB)]
        return jnp.concatenate([total[at:at + NB, :] for at in pieces], axis=1)

    def lead(i, j):
        a = gram_of(i, j)
        if i:
            past = slice(0, i * NB)
            a = a - mm(get(upper_t3, blk(j), past), get(upper3, past, blk(i)))
        return a.T, a

    def link(i, j, a, turned):
        right = mm(get(inverse3, blk(i)), a)
        turned = mm_nt(turned, get(inverse3, blk(i)))
        triangle_ref[blk(i), blk(j)] = right
        put(upper3, (blk(i), blk(j)), right)
        put(upper_t3, (blk(j), blk(i)), turned)

    def early_link(i, j):
        a, turned = lead(i, j)
        link(i, j, split(a), split(turned))

    def early(j):
        i = j - 1
        a, turned = lead(i, j)
        put(ahead3, (0,), a)
        put(ahead3, (1,), turned)
        d = gram_of(j, j)
        if i:
            past = slice(0, i * NB)
            d = d - mm(get(upper_t3, blk(j), past), get(upper3, past, blk(j)))
        work[...] = d

    def late(j):
        i = j - 1
        link(i, j, get(ahead3, 0), get(ahead3, 1))
        work[...] -= mm(get(upper_t3, blk(j), blk(i)), get(upper3, blk(i), blk(j)))

    def projection(j):
        d = cross_of(j)
        if j:
            past = slice(0, j * NB)
            d = d - mm(get(upper_t3, blk(j), past), get(projected3, past))
        return d

    load_slab()
    forward(0)
    for i in range(1, blocks):
        triangle_ref[blk(i), 0:i * NB] = jnp.zeros((NB, i * NB), F32)

    def project(j):
        out = mm(get(inverse3, blk(j)), split(projection(j)))
        projected_ref[blk(j), :] = out
        put(projected3, (blk(j),), out)

    def need(task, names, *args):
        for name in names:
            ensure(name)
        task(*args)

    for j in range(1, blocks):
        for i in range(j - 1):
            add(16 * j + (-3 if j == 2 else -5) + 2 * i, need, early_link, [("gram", j)], i, j)
        add(16 * j - 1.5, need, early, [("gram", j)], j)
        if j < last:
            add(16 * j + (15 if j == 1 else 4), need, project, [("cross", max(j - 1, 1))], j - 1)
    queue.sort(key=lambda x: x[0])

    for j in range(blocks):
        ensure(("gram", j))
        if j:
            pump(16 * j - 1)
            late(j)
        else:
            work[...] = gram_of(0, 0)
        if j < last:
            factor_block([work[SUB * g:SUB * (g + 1), :] for g in range(NB // SUB)],
                         triangle_ref, inverse, j * NB, j * NB, lambda b: pump(16 * j + b))
            done = inverse[blk(j), :]
            put(inverse3, (blk(j),), done)
            put(inverse_t3, (blk(j),), done.T)
    while queue:
        queue.pop(0)[1]()
    together(panel.at[:, pl.ds(0, (pairs - 1) * rows)], 0, 0).wait_send()
    together(panel.at[:, pl.ds(0, pairs * rows)], 1, 0).wait_send()


def last_kernel(triangle_in, projected_in, work, total, panel, panel3, slab, upper3, upper_t3,
                inverse3, inverse_t3, projected3, triangle_ref, projected_ref, remainder_ref,
                corner, inverse, projected, remainder, fresh3, both3, y3, last3, sems):
    blocks, size, _ = panel.shape
    n = slab.shape[1]
    last = blocks - 1
    where, _, _ = packing(blocks * NB, n)
    copies = []

    def send(source, target):
        copies.append(pltpu.make_async_copy(source, target, sems.at[len(copies)]))
        copies[-1].start()

    send(triangle_in.at[0:last * NB], triangle_ref.at[0:last * NB])
    send(triangle_in.at[blk(last), 0:last * NB], triangle_ref.at[blk(last), 0:last * NB])
    if last > 1:
        send(projected_in.at[0:(last - 1) * NB], projected_ref.at[0:(last - 1) * NB])

    def projection(j, before):
        pieces = [where["cross", j, q] for q in range(n // NB)]
        d = jnp.concatenate([total[at:at + NB, :] for at in pieces], axis=1)
        return d - mm(get(upper_t3, blk(j), slice(0, j * NB)), before) if j else d

    def project():
        j = last - 1
        out = mm(get(inverse3, blk(j)), split(projection(j, get(projected3, slice(0, j * NB)))))
        projected[blk(j), :] = out
        put(fresh3, (), out)
        send(projected.at[blk(j)], projected_ref.at[blk(j)])

    def project_last():
        j = last - 1
        before = [jnp.concatenate([projected3[s, 0:j * NB], fresh3[s]], axis=0) if j else fresh3[s]
                  for s in range(3)]
        put(last3, (), projection(last, before))

    def solve_back(k):
        own = projected if k == last - 1 else projected_in
        rhs = jnp.concatenate([own[blk(k), :], triangle_in[blk(k), blk(last)]], axis=1)
        if k + 1 < last:
            after = slice((k + 1) * NB, last * NB)
            rhs = rhs - mm(get(upper3, blk(k), after), get(both3, after))
        put(both3, (blk(k),), mm(get(inverse_t3, blk(k)), split(rhs)))

    def reduce_rest(at):
        rest = jnp.concatenate([slab[at, :], panel[last, at, :]], axis=1)
        if last:
            before = [jnp.concatenate([panel3[s, k, at, :] for k in range(last)], axis=1)
                      for s in range(3)]
            rest = rest - mm(before, get(both3, slice(0, last * NB)))
        remainder[at, :] = rest[:, 0:n]
        put(y3, (at,), rest[:, n:n + NB])

    tasks = {}
    if last:
        tasks[1] = [project, project_last]
    for k in range(last):
        tasks.setdefault(2 + 2 * k, []).append(functools.partial(solve_back, last - 1 - k))
    for r in range(0, size, NB):
        tasks.setdefault(min(4 + 2 * last + 2 * (r // NB), 15), []).append(
            functools.partial(reduce_rest, slice(r, r + NB)))
    if not last:
        put(last3, (), projection(0, None))

    def hook(b):
        for task in tasks.get(b, []):
            task()

    factor_block([work[SUB * g:SUB * (g + 1), :] for g in range(NB // SUB)], corner, inverse, 0, 0, hook)
    send(corner, triangle_ref.at[blk(last), blk(last)])
    done = split(inverse[...])
    out = mm(done, get(last3))
    projected[blk(last), :] = out
    send(projected.at[blk(last)], projected_ref.at[blk(last)])
    part = split(out)
    for at in (slice(0, size // 2), slice(size // 2, size)):
        basis = mm_nt(get(y3, at), done)
        remainder[at, :] = remainder[at, :] - mm(split(basis), part)
        send(remainder.at[at], remainder_ref.at[at])
    for copy in copies:
        copy.wait()


def on_device(mesh, panel_block, trailing):
    halves, groups, devs = (mesh.shape[name] for name in ("half", "grp", "dev"))
    rows, p = panel_block.shape
    size, n = trailing.shape
    blocks = p // NB
    _, stretch, length = packing(p, n)
    levels = (halves * groups).bit_length() - 1
    vmem, dma = pltpu.VMEM, pltpu.SemaphoreType.DMA
    space = pl.BlockSpec(memory_space=pl.ANY)
    inside = pl.BlockSpec(memory_space=pltpu.VMEM)
    kept = (
        vmem((p, p), F32), vmem((p, n), F32), vmem((NB, NB), F32), vmem((length, NB), F32),
        vmem((blocks, size, NB), F32), vmem((3, blocks, size, NB), BF16), vmem((size, n), F32),
        vmem((3, p, p), BF16), vmem((3, p, p), BF16), vmem((3, p, NB), BF16), vmem((3, p, NB), BF16),
        vmem((3, p, n), BF16),
    )
    found = pl.pallas_call(
        functools.partial(lead_kernel, halves, groups, devs),
        out_shape=kept,
        in_specs=[space] * 2,
        out_specs=(inside,) * len(kept),
        scratch_shapes=[
            vmem((levels + 1, length // 2, NB), F32),
            vmem((3, 2, NB, NB), BF16),
            vmem((p, NB), F32),
            vmem((3, p, size), BF16),
            vmem((3, size, n), BF16),
            dma((2,)), dma((2,)), dma((blocks, devs // 2 - 1)), dma((blocks,)),
            dma((levels + 1, len(stretch))), dma((levels + 1, len(stretch))),
        ],
        compiler_params=pltpu.CompilerParams(
            collective_id=0, has_side_effects=True, vmem_limit_bytes=LIMIT),
        name="lead_blocks",
    )(*(pltpu.with_memory_space_constraint(x, pltpu.HBM) for x in (panel_block, trailing)))
    return pl.pallas_call(
        last_kernel,
        out_shape=(
            jax.ShapeDtypeStruct((p, p), F32),
            jax.ShapeDtypeStruct((p, n), F32),
            jax.ShapeDtypeStruct((size, n), F32),
        ),
        in_specs=[inside] * len(kept),
        out_specs=(space,) * 3,
        scratch_shapes=[
            vmem((NB, NB), F32), vmem((NB, NB), F32), vmem((p, n), F32), vmem((size, n), F32),
            vmem((3, NB, n), BF16), vmem((3, p, n + NB), BF16), vmem((3, size, NB), BF16),
            vmem((3, NB, n), BF16), dma((8,)),
        ],
        compiler_params=pltpu.CompilerParams(vmem_limit_bytes=LIMIT),
        name="last_block",
    )(*(pltpu.with_memory_space_constraint(x, pltpu.VMEM) for x in found))


def solution(mesh):
    placed = (P(("half", "grp", "dev"), None), P(("half", "grp"), "dev"))
    return jax.shard_map(
        functools.partial(on_device, mesh),
        mesh=mesh,
        in_specs=placed,
        out_specs=(P(), P(None, "dev"), P(("half", "grp"), "dev")),
        check_vma=False,
    )
```

```python
import functools

import jax
import jax.numpy as jnp
from jax import lax
from jax.experimental import pallas as pl
from jax.experimental.pallas import tpu as pltpu
from jax.sharding import PartitionSpec as P

NB = 128
SUB = 8
LIMIT = 24 << 20
PAIR = 2
F32 = jnp.float32
BF16 = jnp.bfloat16
LEFT = (0, 0, 1, 0, 1, 2)
RIGHT = (0, 1, 0, 2, 1, 0)


PLACES = {
    ("gram", 0): ((-12, -12), -10, -7, -5),
    ("gram", 1): ((-6, -6), 1, 15.3, 15.9),
    ("cross", 1): ((1.1,), 5.5, 22, 30),
    ("gram", 2): ((6, 7), 13, 22.1, 28),
    ("gram", 3): ((15, 15.4), 18, 38, 43),
    ("cross", 2): ((20,), 31.2, 43.1, 47),
    ("cross", 3): ((21,), 31.3, 43.2, 47.1),
}

FORWARDS = (0, -11, -9, 0)


def split(x):
    high = x.astype(BF16)
    rest = x - high.astype(F32)
    middle = rest.astype(BF16)
    low = (rest - middle.astype(F32)).astype(BF16)
    return high, middle, low


def wide(parts, which, axis):
    return jnp.concatenate([parts[s] for s in which], axis=axis)


def contract(a, b, dim):
    return lax.dot_general(a, b, (((1,), (dim,)), ((), ())), preferred_element_type=F32)


def mm(a, b):
    return contract(wide(a, LEFT, 1), wide(b, RIGHT, 0), 0)


def mm_nt(a, b):
    return contract(wide(a, LEFT, 1), wide(b, RIGHT, 1), 1)


def blk(i):
    return slice(i * NB, (i + 1) * NB)


def put(ref, at, x):
    for s, part in enumerate(split(x)):
        ref[(s, *at)] = part


def get(ref, *at):
    return [ref[(s, *at)] for s in range(3)]


def lanes_of(x, at):
    return jnp.take_along_axis(x, jnp.full(x.shape, at, jnp.int32), axis=1)


def factor_block(block, upper_ref, inverse_ref, row0, col0, hook):
    tile = (SUB, NB)
    lane = lax.broadcasted_iota(jnp.int32, tile, 1)
    row = lax.broadcasted_iota(jnp.int32, tile, 0)
    here = [row == j for j in range(SUB)]
    block = list(block)
    groups = len(block)
    ups, lows = [], []
    following = None

    def one(x, at):
        return jnp.broadcast_to(x[at:at + 1, :], tile)

    for b in range(groups):
        hook(b)
        c0 = SUB * b
        own = block[b]
        near = min(groups, (b // PAIR + 2) * PAIR)
        inside = (lane >= c0) & (lane < c0 + SUB)
        opens = b % PAIR == 0
        cols = [lanes_of(own, c0 + t) for t in range(SUB)] if opens else following
        columns = {g: [lanes_of(block[g], c0 + t) for t in range(SUB)] for g in range(b + 1, near)}
        if opens:
            following = [lanes_of(block[b + 1], c0 + SUB + t) for t in range(SUB)]
            below = list(columns[b + 1])
        v = jnp.where(inside, jnp.where(lane == row + c0, 1.0, 0.0), own)
        w = own
        up = low = None
        raw = list(cols)
        for j in range(SUB):
            top = [one(raw[t], j) if t >= j else None for t in range(SUB)]
            rs = lax.rsqrt(top[j])
            r = rs * rs
            e = cols[j] * r
            vj, wj = one(v, j), one(w, j)
            vs, ws = vj * rs, wj * rs
            up = ws if j == 0 else jnp.where(here[j], ws, up)
            low = vs if j == 0 else jnp.where(here[j], vs, low)
            v = jnp.where(here[j], vj * r, v - e * vj)
            if j + 1 < SUB:
                w = w - e * wj
            for t in range(j + 1, SUB):
                raw[t] = cols[t] - (cols[j] * top[t]) * r
                cols[t] = jnp.where(here[j], top[t] * r, raw[t])
            if opens:
                share = below[j] * r
                for t in range(SUB):
                    following[t] = following[t] - share * one(below[j], t)
                for t in range(j + 1, SUB):
                    below[t] = below[t] - (below[j] * top[t]) * r
        up = jnp.where(lane >= row + c0, up, 0.0)
        low = jnp.where(lane <= row + c0, low, 0.0)
        upper_ref[row0 + c0:row0 + c0 + SUB, col0:col0 + NB] = up
        inverse_ref[row0 + c0:row0 + c0 + SUB, :] = low
        ups.append(up)
        lows.append(low)
        if b + 1 < near:
            vt = [one(v, t) for t in range(SUB)]
        for g in range(b + 1, near):
            terms = [columns[g][t] * vt[t] for t in range(SUB)]
            while len(terms) > 1:
                terms = [terms[i] + terms[i + 1] for i in range(0, len(terms), 2)]
            block[g] = jnp.where(inside, 0.0, block[g]) - terms[0]
        if not opens and near < groups:
            end = c0 + SUB
            past = lane >= end
            us = jnp.concatenate([jnp.where(past, u, 0.0) for u in ups[-PAIR:]], axis=0)
            vs = jnp.concatenate(
                [jnp.where(past, u, x) for u, x in zip(ups[-PAIR:], lows[-PAIR:])], axis=0)
            res = lax.dot_general(
                wide(split(us), LEFT, 0), wide(split(vs), RIGHT, 0), (((0,), (0,)), ((), ())),
                preferred_element_type=F32)
            done = (lane >= end - PAIR * SUB) & (lane < end)
            for g in range(near, groups):
                block[g] = jnp.where(done, 0.0, block[g]) - res[SUB * g:SUB * (g + 1), :]


def packing(p, n):
    blocks = p // NB
    regions = [("gram", (0,))]
    for j in range(1, blocks):
        regions.append(("gram", (j,)))
        regions.append(("cross", (0, 1) if j == 1 else (j,)))
    if blocks == 1:
        regions.append(("cross", (0,)))
    where, stretch = {}, {}
    at = 0
    for kind, members in regions:
        first = at
        for j in members:
            for i in range(j + 1 if kind == "gram" else n // NB):
                where[(kind, i, j) if kind == "gram" else (kind, j, i)] = at
                at += NB
        stretch[kind, members[-1]] = (first, at - first)
    return where, stretch, at


def lead_kernel(halves, groups, devs, panel_hbm, trailing_hbm, triangle_ref, projected_ref, work,
                total, panel, panel3, slab, upper3, upper_t3, inverse3, inverse_t3, projected3,
                inbox, ahead3, inverse, turned3, slab3, l_sem, s_sem, a_recv, b_recv, r_send, r_recv):
    mesh_ids = pl.DeviceIdType.MESH
    mine = lax.axis_index("dev")
    rank = lax.axis_index("half") * groups + lax.axis_index("grp")
    pairs = devs // 2
    pair, parity = mine // 2, mine % 2
    levels = (halves * groups).bit_length() - 1
    blocks, size, _ = panel.shape
    rows = size // devs
    p = blocks * NB
    n = slab.shape[1]
    last = blocks - 1
    where, stretch, _ = packing(p, n)

    def slot(dev):
        return pl.ds(pl.multiple_of(dev * rows, rows), rows)

    def same(step):
        return ((pair + step) % pairs) * 2 + parity

    def at_rank(level):
        bit = 1 << level
        other = rank + bit * (1 - 2 * ((rank // bit) % 2))
        return {"half": other // groups, "grp": other % groups}

    for j in range(blocks):
        pltpu.make_async_copy(panel_hbm.at[:, blk(j)], panel.at[j, slot(mine)], l_sem.at[0]).start()
    slab_load = pltpu.make_async_copy(trailing_hbm, slab, l_sem.at[1])
    slab_load.start()

    beside = pair * 2 + 1 - parity
    peers = [{"dev": same(step)} for step in range(1, pairs)] + [{"dev": beside}]
    peers += [at_rank(level) for level in range(levels)]
    barrier = pltpu.get_barrier_semaphore()
    for peer in peers:
        pl.semaphore_signal(barrier, inc=1, device_id=peer, device_id_type=mesh_ids)
    pl.semaphore_wait(barrier, len(peers))

    def arrival(j, step):
        return pltpu.make_async_remote_copy(
            src_ref=panel.at[j, slot(mine)], dst_ref=panel.at[j, slot(mine)],
            send_sem=s_sem.at[0], recv_sem=a_recv.at[j, step - 1],
            device_id={"dev": same(step)}, device_id_type=mesh_ids)

    def passing(j, step):
        owner = same(pairs - step)
        return pltpu.make_async_remote_copy(
            src_ref=panel.at[j, slot(owner)], dst_ref=panel.at[j, slot(owner)],
            send_sem=s_sem.at[1], recv_sem=b_recv.at[j],
            device_id={"dev": beside}, device_id_type=mesh_ids)

    def send(j):
        if j < blocks:
            for step in range(1, pairs):
                arrival(j, step).start()

    own = panel.at[:, slot(mine)]
    pltpu.make_async_copy(own, own, l_sem.at[0]).wait()
    send(0)
    passing(0, 0).start()

    def forward(j):
        near = jnp.minimum(pair, pairs - 1 - pair)
        far = jnp.where(pair < pairs - 1 - pair, 1, -1)
        for k in range(pairs - 1):
            offset = jnp.where(k < 2 * near, (k // 2 + 1) * (1 - 2 * (k % 2)), (k - near + 1) * far)
            step = (pairs - offset) % pairs
            arrival(j, step).wait_recv()
            passing(j, step).start()
            if j == 0 and k == 1:
                send(1)
        send(j + 2)
        if j + 1 < blocks:
            passing(j + 1, 0).start()

    names = list(stretch)

    def reduction(name, level):
        begin, count = stretch[name]
        which = names.index(name)
        half = count // 2
        low = begin + (rank % 2) * half
        keep = pl.ds(pl.multiple_of(low, 8), half)
        give = pl.ds(pl.multiple_of(2 * begin + half - low, 8), half)
        copy = pltpu.make_async_remote_copy(
            src_ref=total.at[keep if level else give],
            dst_ref=inbox.at[level, pl.ds(begin // 2, half)],
            send_sem=r_send.at[level, which], recv_sem=r_recv.at[level, which],
            device_id=at_rank(level if level < levels else 0), device_id_type=mesh_ids)
        return copy, keep, give, slice(begin // 2, begin // 2 + half)

    def together(part, which, at):
        return pltpu.make_async_remote_copy(
            src_ref=part, dst_ref=part, send_sem=s_sem.at[which], recv_sem=b_recv.at[at],
            device_id={"dev": beside}, device_id_type=mesh_ids)

    def arrive(j):
        together(panel.at[j, pl.ds(0, pairs * rows)], 1, j).wait_recv()

    def prepare(j):
        x = panel[j]
        for s, part in enumerate(split(x)):
            panel3[s, j] = part
        for s, part in enumerate(split(x.T)):
            turned3[s, blk(j), :] = part

    def products(j):
        right = [jnp.concatenate([*(panel3[s, i] for i in range(j + 1)), slab3[s]], axis=1)
                 for s in range(3)]
        out = mm([turned3[s, blk(j), :] for s in range(3)], right)
        for i in range(j + 1):
            at = where["gram", i, j]
            total[at:at + NB, :] = out[:, blk(i)]
        for q in range(n // NB):
            at = where["cross", j, q]
            total[at:at + NB, :] = out[:, blk(j + 1 + q)]

    def begin(name):
        reduction(name, 0)[0].start()

    def receive(j):
        arrive(j)
        prepare(j)

    def load_slab():
        slab_load.wait()
        for s, part in enumerate(split(slab[...])):
            slab3[s] = part

    def advance(name, level):
        copy, keep, give, place = reduction(name, level)
        copy.wait()
        if level < levels:
            total[keep, :] += inbox[level, place]
            reduction(name, level + 1)[0].start()
        else:
            total[give, :] = inbox[level, place]
            ready.add(name)

    queue = []

    def add(place, task, *args):
        queue.append((place, functools.partial(task, *args)))

    for j in range(1, blocks):
        add(FORWARDS[min(j, 3)], forward, j)
    for name in names:
        kind, j = name
        start, *at = PLACES.get(name, ((48, 48), 49, 50, 51))
        if kind == "gram":
            add(start[0], receive, j)
            add(start[1], products, j)
        add(start[-1], begin, name)
        for level in range(levels + 1):
            add(at[0 if level == 0 else 2 if level == levels else 1], advance, name, level)
    ready = set()

    def pump(place):
        while queue and queue[0][0] <= place:
            queue.pop(0)[1]()

    def ensure(name):
        at = 0
        while name not in ready:
            while queue[at][1].func is need:
                at += 1
            queue.pop(at)[1]()

    def gram_of(i, j):
        at = where["gram", i, j]
        return total[at:at + NB, :]

    def cross_of(i):
        pieces = [where["cross", i, q] for q in range(n // NB)]
        return jnp.concatenate([total[at:at + NB, :] for at in pieces], axis=1)

    def lead(i, j):
        a = gram_of(i, j)
        if i:
            past = slice(0, i * NB)
            a = a - mm(get(upper_t3, blk(j), past), get(upper3, past, blk(i)))
        return a.T, a

    def link(i, j, a, turned):
        right = mm(get(inverse3, blk(i)), a)
        turned = mm_nt(turned, get(inverse3, blk(i)))
        triangle_ref[blk(i), blk(j)] = right
        put(upper3, (blk(i), blk(j)), right)
        put(upper_t3, (blk(j), blk(i)), turned)

    def early_link(i, j):
        a, turned = lead(i, j)
        link(i, j, split(a), split(turned))

    def early(j):
        i = j - 1
        a, turned = lead(i, j)
        put(ahead3, (0,), a)
        put(ahead3, (1,), turned)
        d = gram_of(j, j)
        if i:
            past = slice(0, i * NB)
            d = d - mm(get(upper_t3, blk(j), past), get(upper3, past, blk(j)))
        work[...] = d

    def late(j):
        i = j - 1
        link(i, j, get(ahead3, 0), get(ahead3, 1))
        work[...] -= mm(get(upper_t3, blk(j), blk(i)), get(upper3, blk(i), blk(j)))

    def projection(j):
        d = cross_of(j)
        if j:
            past = slice(0, j * NB)
            d = d - mm(get(upper_t3, blk(j), past), get(projected3, past))
        return d

    load_slab()
    forward(0)
    for i in range(1, blocks):
        triangle_ref[blk(i), 0:i * NB] = jnp.zeros((NB, i * NB), F32)

    def project(j):
        out = mm(get(inverse3, blk(j)), split(projection(j)))
        projected_ref[blk(j), :] = out
        put(projected3, (blk(j),), out)

    def need(task, names, *args):
        for name in names:
            ensure(name)
        task(*args)

    for j in range(1, blocks):
        for i in range(j - 1):
            add(16 * j + (-3 if j == 2 else -5) + 2 * i, need, early_link, [("gram", j)], i, j)
        add(16 * j - 1.5, need, early, [("gram", j)], j)
        if j < last:
            add(16 * j + (15 if j == 1 else 4), need, project, [("cross", max(j - 1, 1))], j - 1)
    queue.sort(key=lambda x: x[0])

    for j in range(blocks):
        ensure(("gram", j))
        if j:
            pump(16 * j - 1)
            late(j)
        else:
            work[...] = gram_of(0, 0)
        if j < last:
            factor_block([work[SUB * g:SUB * (g + 1), :] for g in range(NB // SUB)],
                         triangle_ref, inverse, j * NB, j * NB, lambda b: pump(16 * j + b))
            done = inverse[blk(j), :]
            put(inverse3, (blk(j),), done)
            put(inverse_t3, (blk(j),), done.T)
    while queue:
        queue.pop(0)[1]()
    together(panel.at[:, pl.ds(0, (pairs - 1) * rows)], 0, 0).wait_send()
    together(panel.at[:, pl.ds(0, pairs * rows)], 1, 0).wait_send()


def last_kernel(triangle_in, projected_in, work, total, panel, panel3, slab, upper3, upper_t3,
                inverse3, inverse_t3, projected3, triangle_ref, projected_ref, remainder_ref,
                corner, inverse, projected, remainder, fresh3, both3, y3, last3, sems):
    blocks, size, _ = panel.shape
    n = slab.shape[1]
    last = blocks - 1
    where, _, _ = packing(blocks * NB, n)
    copies = []

    def send(source, target):
        copies.append(pltpu.make_async_copy(source, target, sems.at[len(copies)]))
        copies[-1].start()

    send(triangle_in.at[0:last * NB], triangle_ref.at[0:last * NB])
    send(triangle_in.at[blk(last), 0:last * NB], triangle_ref.at[blk(last), 0:last * NB])
    if last > 1:
        send(projected_in.at[0:(last - 1) * NB], projected_ref.at[0:(last - 1) * NB])

    def projection(j, before):
        pieces = [where["cross", j, q] for q in range(n // NB)]
        d = jnp.concatenate([total[at:at + NB, :] for at in pieces], axis=1)
        return d - mm(get(upper_t3, blk(j), slice(0, j * NB)), before) if j else d

    def project():
        j = last - 1
        out = mm(get(inverse3, blk(j)), split(projection(j, get(projected3, slice(0, j * NB)))))
        projected[blk(j), :] = out
        put(fresh3, (), out)
        send(projected.at[blk(j)], projected_ref.at[blk(j)])

    def project_last():
        j = last - 1
        before = [jnp.concatenate([projected3[s, 0:j * NB], fresh3[s]], axis=0) if j else fresh3[s]
                  for s in range(3)]
        put(last3, (), projection(last, before))

    def solve_back(k):
        own = projected if k == last - 1 else projected_in
        rhs = jnp.concatenate([own[blk(k), :], triangle_in[blk(k), blk(last)]], axis=1)
        if k + 1 < last:
            after = slice((k + 1) * NB, last * NB)
            rhs = rhs - mm(get(upper3, blk(k), after), get(both3, after))
        put(both3, (blk(k),), mm(get(inverse_t3, blk(k)), split(rhs)))

    def reduce_rest(at):
        rest = jnp.concatenate([slab[at, :], panel[last, at, :]], axis=1)
        if last:
            before = [jnp.concatenate([panel3[s, k, at, :] for k in range(last)], axis=1)
                      for s in range(3)]
            rest = rest - mm(before, get(both3, slice(0, last * NB)))
        remainder[at, :] = rest[:, 0:n]
        put(y3, (at,), rest[:, n:n + NB])

    tasks = {}
    if last:
        tasks[1] = [project, project_last]
    for k in range(last):
        tasks.setdefault(2 + 2 * k, []).append(functools.partial(solve_back, last - 1 - k))
    for r in range(0, size, NB):
        tasks.setdefault(min(4 + 2 * last + 2 * (r // NB), 15), []).append(
            functools.partial(reduce_rest, slice(r, r + NB)))
    if not last:
        put(last3, (), projection(0, None))

    def hook(b):
        for task in tasks.get(b, []):
            task()

    factor_block([work[SUB * g:SUB * (g + 1), :] for g in range(NB // SUB)], corner, inverse, 0, 0, hook)
    send(corner, triangle_ref.at[blk(last), blk(last)])
    done = split(inverse[...])
    out = mm(done, get(last3))
    projected[blk(last), :] = out
    send(projected.at[blk(last)], projected_ref.at[blk(last)])
    part = split(out)
    for at in (slice(0, size // 2), slice(size // 2, size)):
        basis = mm_nt(get(y3, at), done)
        remainder[at, :] = remainder[at, :] - mm(split(basis), part)
        send(remainder.at[at], remainder_ref.at[at])
    for copy in copies:
        copy.wait()


def on_device(mesh, panel_block, trailing):
    halves, groups, devs = (mesh.shape[name] for name in ("half", "grp", "dev"))
    rows, p = panel_block.shape
    size, n = trailing.shape
    blocks = p // NB
    _, stretch, length = packing(p, n)
    levels = (halves * groups).bit_length() - 1
    vmem, dma = pltpu.VMEM, pltpu.SemaphoreType.DMA
    space = pl.BlockSpec(memory_space=pl.ANY)
    inside = pl.BlockSpec(memory_space=pltpu.VMEM)
    kept = (
        vmem((p, p), F32), vmem((p, n), F32), vmem((NB, NB), F32), vmem((length, NB), F32),
        vmem((blocks, size, NB), F32), vmem((3, blocks, size, NB), BF16), vmem((size, n), F32),
        vmem((3, p, p), BF16), vmem((3, p, p), BF16), vmem((3, p, NB), BF16), vmem((3, p, NB), BF16),
        vmem((3, p, n), BF16),
    )
    found = pl.pallas_call(
        functools.partial(lead_kernel, halves, groups, devs),
        out_shape=kept,
        in_specs=[space] * 2,
        out_specs=(inside,) * len(kept),
        scratch_shapes=[
            vmem((levels + 1, length // 2, NB), F32),
            vmem((3, 2, NB, NB), BF16),
            vmem((p, NB), F32),
            vmem((3, p, size), BF16),
            vmem((3, size, n), BF16),
            dma((2,)), dma((2,)), dma((blocks, devs // 2 - 1)), dma((blocks,)),
            dma((levels + 1, len(stretch))), dma((levels + 1, len(stretch))),
        ],
        compiler_params=pltpu.CompilerParams(
            collective_id=0, has_side_effects=True, vmem_limit_bytes=LIMIT),
        name="lead_blocks",
    )(*(pltpu.with_memory_space_constraint(x, pltpu.HBM) for x in (panel_block, trailing)))
    return pl.pallas_call(
        last_kernel,
        out_shape=(
            jax.ShapeDtypeStruct((p, p), F32),
            jax.ShapeDtypeStruct((p, n), F32),
            jax.ShapeDtypeStruct((size, n), F32),
        ),
        in_specs=[inside] * len(kept),
        out_specs=(space,) * 3,
        scratch_shapes=[
            vmem((NB, NB), F32), vmem((NB, NB), F32), vmem((p, n), F32), vmem((size, n), F32),
            vmem((3, NB, n), BF16), vmem((3, p, n + NB), BF16), vmem((3, size, NB), BF16),
            vmem((3, NB, n), BF16), dma((8,)),
        ],
        compiler_params=pltpu.CompilerParams(vmem_limit_bytes=LIMIT),
        name="last_block",
    )(*(pltpu.with_memory_space_constraint(x, pltpu.VMEM) for x in found))


def solution(mesh):
    placed = (P(("half", "grp", "dev"), None), P(("half", "grp"), "dev"))
    return jax.shard_map(
        functools.partial(on_device, mesh),
        mesh=mesh,
        in_specs=placed,
        out_specs=(P(), P(None, "dev"), P(("half", "grp"), "dev")),
        check_vma=False,
    )
```

```python
import functools

import jax
import jax.numpy as jnp
from jax import lax
from jax.experimental import pallas as pl
from jax.experimental.pallas import tpu as pltpu
from jax.sharding import PartitionSpec as P

NB = 128
SUB = 8
LIMIT = 24 << 20
PAIR = 2
F32 = jnp.float32
BF16 = jnp.bfloat16
LEFT = (0, 0, 1, 0, 1, 2)
RIGHT = (0, 1, 0, 2, 1, 0)


PLACES = {
    ("gram", 0): ((-12, -12), -10, -7, -5),
    ("gram", 1): ((-6, -6), 1, 15.3, 15.9),
    ("cross", 1): ((1.1,), 5.5, 22, 30),
    ("gram", 2): ((6, 7), 13, 22.1, 28),
    ("gram", 3): ((15, 15.4), 18, 38, 43),
    ("cross", 2): ((20,), 31.2, 43.1, 47),
    ("cross", 3): ((21,), 31.3, 43.2, 47.1),
}

FORWARDS = (0, -11, -9, 0)


def split(x):
    high = x.astype(BF16)
    rest = x - high.astype(F32)
    middle = rest.astype(BF16)
    low = (rest - middle.astype(F32)).astype(BF16)
    return high, middle, low


def wide(parts, which, axis):
    return jnp.concatenate([parts[s] for s in which], axis=axis)


def contract(a, b, dim):
    return lax.dot_general(a, b, (((1,), (dim,)), ((), ())), preferred_element_type=F32)


def mm(a, b):
    return contract(wide(a, LEFT, 1), wide(b, RIGHT, 0), 0)


def mm_nt(a, b):
    return contract(wide(a, LEFT, 1), wide(b, RIGHT, 1), 1)


def blk(i):
    return slice(i * NB, (i + 1) * NB)


def put(ref, at, x):
    for s, part in enumerate(split(x)):
        ref[(s, *at)] = part


def get(ref, *at):
    return [ref[(s, *at)] for s in range(3)]


def lanes_of(x, at):
    return jnp.take_along_axis(x, jnp.full(x.shape, at, jnp.int32), axis=1)


def factor_block(block, upper_ref, inverse_ref, row0, col0, hook):
    tile = (SUB, NB)
    lane = lax.broadcasted_iota(jnp.int32, tile, 1)
    row = lax.broadcasted_iota(jnp.int32, tile, 0)
    here = [row == j for j in range(SUB)]
    block = list(block)
    groups = len(block)
    ups, lows = [], []
    following = None

    def one(x, at):
        return jnp.broadcast_to(x[at:at + 1, :], tile)

    for b in range(groups):
        hook(b)
        c0 = SUB * b
        own = block[b]
        near = min(groups, (b // PAIR + 2) * PAIR)
        inside = (lane >= c0) & (lane < c0 + SUB)
        opens = b % PAIR == 0
        cols = [lanes_of(own, c0 + t) for t in range(SUB)] if opens else following
        columns = {g: [lanes_of(block[g], c0 + t) for t in range(SUB)] for g in range(b + 1, near)}
        if opens:
            following = [lanes_of(block[b + 1], c0 + SUB + t) for t in range(SUB)]
            below = list(columns[b + 1])
        v = jnp.where(inside, jnp.where(lane == row + c0, 1.0, 0.0), own)
        w = own
        up = low = None
        raw = list(cols)
        for j in range(SUB):
            top = [one(raw[t], j) if t >= j else None for t in range(SUB)]
            rs = lax.rsqrt(top[j])
            r = rs * rs
            e = cols[j] * r
            vj, wj = one(v, j), one(w, j)
            vs, ws = vj * rs, wj * rs
            up = ws if j == 0 else jnp.where(here[j], ws, up)
            low = vs if j == 0 else jnp.where(here[j], vs, low)
            v = jnp.where(here[j], vj * r, v - e * vj)
            if j + 1 < SUB:
                w = w - e * wj
            for t in range(j + 1, SUB):
                raw[t] = cols[t] - (cols[j] * top[t]) * r
                cols[t] = jnp.where(here[j], top[t] * r, raw[t])
            if opens:
                share = below[j] * r
                for t in range(SUB):
                    following[t] = following[t] - share * one(below[j], t)
                for t in range(j + 1, SUB):
                    below[t] = below[t] - (below[j] * top[t]) * r
        up = jnp.where(lane >= row + c0, up, 0.0)
        low = jnp.where(lane <= row + c0, low, 0.0)
        upper_ref[row0 + c0:row0 + c0 + SUB, col0:col0 + NB] = up
        inverse_ref[row0 + c0:row0 + c0 + SUB, :] = low
        ups.append(up)
        lows.append(low)
        if b + 1 < near:
            vt = [one(v, t) for t in range(SUB)]
        for g in range(b + 1, near):
            terms = [columns[g][t] * vt[t] for t in range(SUB)]
            while len(terms) > 1:
                terms = [terms[i] + terms[i + 1] for i in range(0, len(terms), 2)]
            block[g] = jnp.where(inside, 0.0, block[g]) - terms[0]
        if not opens and near < groups:
            end = c0 + SUB
            past = lane >= end
            us = jnp.concatenate([jnp.where(past, u, 0.0) for u in ups[-PAIR:]], axis=0)
            vs = jnp.concatenate(
                [jnp.where(past, u, x) for u, x in zip(ups[-PAIR:], lows[-PAIR:])], axis=0)
            res = lax.dot_general(
                wide(split(us), LEFT, 0), wide(split(vs), RIGHT, 0), (((0,), (0,)), ((), ())),
                preferred_element_type=F32)
            done = (lane >= end - PAIR * SUB) & (lane < end)
            for g in range(near, groups):
                block[g] = jnp.where(done, 0.0, block[g]) - res[SUB * g:SUB * (g + 1), :]


def packing(p, n):
    blocks = p // NB
    regions = [("gram", (0,))]
    for j in range(1, blocks):
        regions.append(("gram", (j,)))
        regions.append(("cross", (0, 1) if j == 1 else (j,)))
    if blocks == 1:
        regions.append(("cross", (0,)))
    where, stretch = {}, {}
    at = 0
    for kind, members in regions:
        first = at
        for j in members:
            for i in range(j + 1 if kind == "gram" else n // NB):
                where[(kind, i, j) if kind == "gram" else (kind, j, i)] = at
                at += NB
        stretch[kind, members[-1]] = (first, at - first)
    return where, stretch, at


def lead_kernel(halves, groups, devs, panel_hbm, trailing_hbm, triangle_ref, projected_ref, work,
                total, panel, panel3, slab, upper3, upper_t3, inverse3, inverse_t3, projected3,
                inbox, ahead3, inverse, turned3, slab3, l_sem, s_sem, a_recv, b_recv, r_send, r_recv):
    mesh_ids = pl.DeviceIdType.MESH
    mine = lax.axis_index("dev")
    rank = lax.axis_index("half") * groups + lax.axis_index("grp")
    pairs = devs // 2
    pair, parity = mine // 2, mine % 2
    levels = (halves * groups).bit_length() - 1
    blocks, size, _ = panel.shape
    rows = size // devs
    p = blocks * NB
    n = slab.shape[1]
    last = blocks - 1
    where, stretch, _ = packing(p, n)

    def slot(dev):
        return pl.ds(pl.multiple_of(dev * rows, rows), rows)

    def same(step):
        return ((pair + step) % pairs) * 2 + parity

    def at_rank(level):
        bit = 1 << level
        other = rank + bit * (1 - 2 * ((rank // bit) % 2))
        return {"half": other // groups, "grp": other % groups}

    for j in range(blocks):
        pltpu.make_async_copy(panel_hbm.at[:, blk(j)], panel.at[j, slot(mine)], l_sem.at[0]).start()
    slab_load = pltpu.make_async_copy(trailing_hbm, slab, l_sem.at[1])
    slab_load.start()

    beside = pair * 2 + 1 - parity
    peers = [{"dev": same(step)} for step in range(1, pairs)] + [{"dev": beside}]
    peers += [at_rank(level) for level in range(levels)]
    barrier = pltpu.get_barrier_semaphore()
    for peer in peers:
        pl.semaphore_signal(barrier, inc=1, device_id=peer, device_id_type=mesh_ids)
    pl.semaphore_wait(barrier, len(peers))

    def arrival(j, step):
        return pltpu.make_async_remote_copy(
            src_ref=panel.at[j, slot(mine)], dst_ref=panel.at[j, slot(mine)],
            send_sem=s_sem.at[0], recv_sem=a_recv.at[j, step - 1],
            device_id={"dev": same(step)}, device_id_type=mesh_ids)

    def passing(j, step):
        owner = same(pairs - step)
        return pltpu.make_async_remote_copy(
            src_ref=panel.at[j, slot(owner)], dst_ref=panel.at[j, slot(owner)],
            send_sem=s_sem.at[1], recv_sem=b_recv.at[j],
            device_id={"dev": beside}, device_id_type=mesh_ids)

    def send(j):
        if j < blocks:
            for step in range(1, pairs):
                arrival(j, step).start()

    own = panel.at[:, slot(mine)]
    pltpu.make_async_copy(own, own, l_sem.at[0]).wait()
    send(0)
    passing(0, 0).start()

    def forward(j):
        near = jnp.minimum(pair, pairs - 1 - pair)
        far = jnp.where(pair < pairs - 1 - pair, 1, -1)
        for k in range(pairs - 1):
            offset = jnp.where(k < 2 * near, (k // 2 + 1) * (1 - 2 * (k % 2)), (k - near + 1) * far)
            step = (pairs - offset) % pairs
            arrival(j, step).wait_recv()
            passing(j, step).start()
            if j == 0 and k == 1:
                send(1)
        send(j + 2)
        if j + 1 < blocks:
            passing(j + 1, 0).start()

    names = list(stretch)

    def reduction(name, level):
        begin, count = stretch[name]
        which = names.index(name)
        half = count // 2
        low = begin + (rank % 2) * half
        keep = pl.ds(pl.multiple_of(low, 8), half)
        give = pl.ds(pl.multiple_of(2 * begin + half - low, 8), half)
        copy = pltpu.make_async_remote_copy(
            src_ref=total.at[keep if level else give],
            dst_ref=inbox.at[level, pl.ds(begin // 2, half)],
            send_sem=r_send.at[level, which], recv_sem=r_recv.at[level, which],
            device_id=at_rank(level if level < levels else 0), device_id_type=mesh_ids)
        return copy, keep, give, slice(begin // 2, begin // 2 + half)

    def together(part, which, at):
        return pltpu.make_async_remote_copy(
            src_ref=part, dst_ref=part, send_sem=s_sem.at[which], recv_sem=b_recv.at[at],
            device_id={"dev": beside}, device_id_type=mesh_ids)

    def arrive(j):
        together(panel.at[j, pl.ds(0, pairs * rows)], 1, j).wait_recv()

    def prepare(j):
        x = panel[j]
        for s, part in enumerate(split(x)):
            panel3[s, j] = part
        for s, part in enumerate(split(x.T)):
            turned3[s, blk(j), :] = part

    def products(j):
        right = [jnp.concatenate([*(panel3[s, i] for i in range(j + 1)), slab3[s]], axis=1)
                 for s in range(3)]
        out = mm([turned3[s, blk(j), :] for s in range(3)], right)
        for i in range(j + 1):
            at = where["gram", i, j]
            total[at:at + NB, :] = out[:, blk(i)]
        for q in range(n // NB):
            at = where["cross", j, q]
            total[at:at + NB, :] = out[:, blk(j + 1 + q)]

    def begin(name):
        reduction(name, 0)[0].start()

    def receive(j):
        arrive(j)
        prepare(j)

    def load_slab():
        slab_load.wait()
        for s, part in enumerate(split(slab[...])):
            slab3[s] = part

    def advance(name, level):
        copy, keep, give, place = reduction(name, level)
        copy.wait()
        if level < levels:
            total[keep, :] += inbox[level, place]
            reduction(name, level + 1)[0].start()
        else:
            total[give, :] = inbox[level, place]
            ready.add(name)

    queue = []

    def add(place, task, *args):
        queue.append((place, functools.partial(task, *args)))

    for j in range(1, blocks):
        add(FORWARDS[min(j, 3)], forward, j)
    for name in names:
        kind, j = name
        start, *at = PLACES.get(name, ((48, 48), 49, 50, 51))
        if kind == "gram":
            add(start[0], receive, j)
            add(start[1], products, j)
        add(start[-1], begin, name)
        for level in range(levels + 1):
            add(at[0 if level == 0 else 2 if level == levels else 1], advance, name, level)
    ready = set()

    def pump(place):
        while queue and queue[0][0] <= place:
            queue.pop(0)[1]()

    def ensure(name):
        at = 0
        while name not in ready:
            while queue[at][1].func is need:
                at += 1
            queue.pop(at)[1]()

    def gram_of(i, j):
        at = where["gram", i, j]
        return total[at:at + NB, :]

    def cross_of(i):
        pieces = [where["cross", i, q] for q in range(n // NB)]
        return jnp.concatenate([total[at:at + NB, :] for at in pieces], axis=1)

    def lead(i, j):
        a = gram_of(i, j)
        if i:
            past = slice(0, i * NB)
            a = a - mm(get(upper_t3, blk(j), past), get(upper3, past, blk(i)))
        return a.T, a

    def link(i, j, a, turned):
        right = mm(get(inverse3, blk(i)), a)
        turned = mm_nt(turned, get(inverse3, blk(i)))
        triangle_ref[blk(i), blk(j)] = right
        put(upper3, (blk(i), blk(j)), right)
        put(upper_t3, (blk(j), blk(i)), turned)

    def early_link(i, j):
        a, turned = lead(i, j)
        link(i, j, split(a), split(turned))

    def early(j):
        i = j - 1
        a, turned = lead(i, j)
        put(ahead3, (0,), a)
        put(ahead3, (1,), turned)
        d = gram_of(j, j)
        if i:
            past = slice(0, i * NB)
            d = d - mm(get(upper_t3, blk(j), past), get(upper3, past, blk(j)))
        work[...] = d

    def late(j):
        i = j - 1
        link(i, j, get(ahead3, 0), get(ahead3, 1))
        work[...] -= mm(get(upper_t3, blk(j), blk(i)), get(upper3, blk(i), blk(j)))

    def projection(j):
        d = cross_of(j)
        if j:
            past = slice(0, j * NB)
            d = d - mm(get(upper_t3, blk(j), past), get(projected3, past))
        return d

    load_slab()
    forward(0)
    for i in range(1, blocks):
        triangle_ref[blk(i), 0:i * NB] = jnp.zeros((NB, i * NB), F32)

    def project(j):
        out = mm(get(inverse3, blk(j)), split(projection(j)))
        projected_ref[blk(j), :] = out
        put(projected3, (blk(j),), out)

    def need(task, names, *args):
        for name in names:
            ensure(name)
        task(*args)

    for j in range(1, blocks):
        for i in range(j - 1):
            add(16 * j + (-3 if j == 2 else -5) + 2 * i, need, early_link, [("gram", j)], i, j)
        add(16 * j - 1.5, need, early, [("gram", j)], j)
        if j < last:
            add(16 * j + (15 if j == 1 else 4), need, project, [("cross", max(j - 1, 1))], j - 1)
    queue.sort(key=lambda x: x[0])

    for j in range(blocks):
        ensure(("gram", j))
        if j:
            pump(16 * j - 1)
            late(j)
        else:
            work[...] = gram_of(0, 0)
        if j < last:
            factor_block([work[SUB * g:SUB * (g + 1), :] for g in range(NB // SUB)],
                         triangle_ref, inverse, j * NB, j * NB, lambda b: pump(16 * j + b))
            done = inverse[blk(j), :]
            put(inverse3, (blk(j),), done)
            put(inverse_t3, (blk(j),), done.T)
    while queue:
        queue.pop(0)[1]()
    together(panel.at[:, pl.ds(0, (pairs - 1) * rows)], 0, 0).wait_send()
    together(panel.at[:, pl.ds(0, pairs * rows)], 1, 0).wait_send()


def last_kernel(triangle_in, projected_in, work, total, panel, panel3, slab, upper3, upper_t3,
                inverse3, inverse_t3, projected3, triangle_ref, projected_ref, remainder_ref,
                corner, inverse, projected, remainder, fresh3, both3, y3, last3, sems):
    blocks, size, _ = panel.shape
    n = slab.shape[1]
    last = blocks - 1
    where, _, _ = packing(blocks * NB, n)
    copies = []

    def send(source, target):
        copies.append(pltpu.make_async_copy(source, target, sems.at[len(copies)]))
        copies[-1].start()

    send(triangle_in.at[0:last * NB], triangle_ref.at[0:last * NB])
    send(triangle_in.at[blk(last), 0:last * NB], triangle_ref.at[blk(last), 0:last * NB])
    if last > 1:
        send(projected_in.at[0:(last - 1) * NB], projected_ref.at[0:(last - 1) * NB])

    def projection(j, before):
        pieces = [where["cross", j, q] for q in range(n // NB)]
        d = jnp.concatenate([total[at:at + NB, :] for at in pieces], axis=1)
        return d - mm(get(upper_t3, blk(j), slice(0, j * NB)), before) if j else d

    def project():
        j = last - 1
        out = mm(get(inverse3, blk(j)), split(projection(j, get(projected3, slice(0, j * NB)))))
        projected[blk(j), :] = out
        put(fresh3, (), out)
        send(projected.at[blk(j)], projected_ref.at[blk(j)])

    def project_last():
        j = last - 1
        before = [jnp.concatenate([projected3[s, 0:j * NB], fresh3[s]], axis=0) if j else fresh3[s]
                  for s in range(3)]
        put(last3, (), projection(last, before))

    def solve_back(k):
        own = projected if k == last - 1 else projected_in
        rhs = jnp.concatenate([own[blk(k), :], triangle_in[blk(k), blk(last)]], axis=1)
        if k + 1 < last:
            after = slice((k + 1) * NB, last * NB)
            rhs = rhs - mm(get(upper3, blk(k), after), get(both3, after))
        put(both3, (blk(k),), mm(get(inverse_t3, blk(k)), split(rhs)))

    def reduce_rest(at):
        rest = jnp.concatenate([slab[at, :], panel[last, at, :]], axis=1)
        if last:
            before = [jnp.concatenate([panel3[s, k, at, :] for k in range(last)], axis=1)
                      for s in range(3)]
            rest = rest - mm(before, get(both3, slice(0, last * NB)))
        remainder[at, :] = rest[:, 0:n]
        put(y3, (at,), rest[:, n:n + NB])

    tasks = {}
    if last:
        tasks[1] = [project, project_last]
    for k in range(last):
        tasks.setdefault(2 + 2 * k, []).append(functools.partial(solve_back, last - 1 - k))
    for r in range(0, size, 2 * NB):
        tasks.setdefault(min(4 + 2 * last + 2 * (r // NB), 15), []).append(
            functools.partial(reduce_rest, slice(r, r + 2 * NB)))
    if not last:
        put(last3, (), projection(0, None))

    def hook(b):
        for task in tasks.get(b, []):
            task()

    factor_block([work[SUB * g:SUB * (g + 1), :] for g in range(NB // SUB)], corner, inverse, 0, 0, hook)
    send(corner, triangle_ref.at[blk(last), blk(last)])
    done = split(inverse[...])
    out = mm(done, get(last3))
    projected[blk(last), :] = out
    send(projected.at[blk(last)], projected_ref.at[blk(last)])
    part = split(out)
    for at in (slice(0, size // 2), slice(size // 2, size)):
        basis = mm_nt(get(y3, at), done)
        remainder[at, :] = remainder[at, :] - mm(split(basis), part)
        send(remainder.at[at], remainder_ref.at[at])
    for copy in copies:
        copy.wait()


def on_device(mesh, panel_block, trailing):
    halves, groups, devs = (mesh.shape[name] for name in ("half", "grp", "dev"))
    rows, p = panel_block.shape
    size, n = trailing.shape
    blocks = p // NB
    _, stretch, length = packing(p, n)
    levels = (halves * groups).bit_length() - 1
    vmem, dma = pltpu.VMEM, pltpu.SemaphoreType.DMA
    space = pl.BlockSpec(memory_space=pl.ANY)
    inside = pl.BlockSpec(memory_space=pltpu.VMEM)
    kept = (
        vmem((p, p), F32), vmem((p, n), F32), vmem((NB, NB), F32), vmem((length, NB), F32),
        vmem((blocks, size, NB), F32), vmem((3, blocks, size, NB), BF16), vmem((size, n), F32),
        vmem((3, p, p), BF16), vmem((3, p, p), BF16), vmem((3, p, NB), BF16), vmem((3, p, NB), BF16),
        vmem((3, p, n), BF16),
    )
    found = pl.pallas_call(
        functools.partial(lead_kernel, halves, groups, devs),
        out_shape=kept,
        in_specs=[space] * 2,
        out_specs=(inside,) * len(kept),
        scratch_shapes=[
            vmem((levels + 1, length // 2, NB), F32),
            vmem((3, 2, NB, NB), BF16),
            vmem((p, NB), F32),
            vmem((3, p, size), BF16),
            vmem((3, size, n), BF16),
            dma((2,)), dma((2,)), dma((blocks, devs // 2 - 1)), dma((blocks,)),
            dma((levels + 1, len(stretch))), dma((levels + 1, len(stretch))),
        ],
        compiler_params=pltpu.CompilerParams(
            collective_id=0, has_side_effects=True, vmem_limit_bytes=LIMIT),
        name="lead_blocks",
    )(*(pltpu.with_memory_space_constraint(x, pltpu.HBM) for x in (panel_block, trailing)))
    return pl.pallas_call(
        last_kernel,
        out_shape=(
            jax.ShapeDtypeStruct((p, p), F32),
            jax.ShapeDtypeStruct((p, n), F32),
            jax.ShapeDtypeStruct((size, n), F32),
        ),
        in_specs=[inside] * len(kept),
        out_specs=(space,) * 3,
        scratch_shapes=[
            vmem((NB, NB), F32), vmem((NB, NB), F32), vmem((p, n), F32), vmem((size, n), F32),
            vmem((3, NB, n), BF16), vmem((3, p, n + NB), BF16), vmem((3, size, NB), BF16),
            vmem((3, NB, n), BF16), dma((8,)),
        ],
        compiler_params=pltpu.CompilerParams(vmem_limit_bytes=LIMIT),
        name="last_block",
    )(*(pltpu.with_memory_space_constraint(x, pltpu.VMEM) for x in found))


def solution(mesh):
    placed = (P(("half", "grp", "dev"), None), P(("half", "grp"), "dev"))
    return jax.shard_map(
        functools.partial(on_device, mesh),
        mesh=mesh,
        in_specs=placed,
        out_specs=(P(), P(None, "dev"), P(("half", "grp"), "dev")),
        check_vma=False,
    )
```
